256 devices in a mesh: gx: 16 (over x_lo, y, core), yz: 16 (over z, x_hi).
Axes of the slice: x: 4 (x_hi: 2, x_lo: 2; x = x_hi * 2 + x_lo), y: 4, z: 8, core: 2. Of those that a mesh axis runs over, the one named last changes fastest.
Arguments:
- volume: bfloat16 [128, 16, 128, 128], P('gx', None, 'yz'), may hold values from -6 to 6
- weight_one: bfloat16 [32, 432], replicated, may hold values from -0.875 to 0.875
- weight_two: bfloat16 [64, 864], replicated, may hold values from -0.625 to 0.625
- weight_three: bfloat16 [128, 1728], replicated, may hold values from -0.21875 to 0.21875
Outputs:
- features: bfloat16 [128, 32, 1024], P('yz', 'gx')
The draws below stay inside these ranges and needn't reach their ends.
All inputs are finite; a program needn't handle non-finite values.
Results may differ from the reference program's by a relative error of at most 0.0053.
Values may be sent and summed in bfloat16 or wider, within the bound.
A program may use at most 64 MiB of HBM per device.

```python
import jax
import jax.numpy as jnp
from jax import lax

C1 = 16
C2 = 32
C3 = 64
C4 = 128
NZ = 128
NX = 128
NY = 128


def block_scale(rng, dims, pieces, smallest, top_value):
    factor_of = 1.0
    for position, parts in pieces:
        heights = jax.random.uniform(jax.random.fold_in(jax.random.fold_in(rng, 6), position), (parts,), jnp.float32, smallest / len(pieces), top_value / len(pieces))
        factor_of = factor_of * jnp.repeat(jnp.exp(heights), dims[position] // parts).reshape((-1,) + (1,) * (len(dims) - 1 - position))
    return factor_of


def scatter_about(own_key, extent, spread, bound, cuts=(), kind=jnp.bfloat16):
    drawn = jax.random.normal(own_key, extent, jnp.float32) * spread
    if len(cuts) > 0:
        drawn = block_scale(own_key, extent, cuts, -0.22, 0.18) * drawn
    return jnp.clip(drawn, min=-bound, max=bound).astype(kind)


def setup_inputs(seed: int = 0) -> dict:
    key_of = jax.random.split(jax.random.key(seed), 5)
    return {
        "volume": scatter_about(key_of[0], (NX, C1, NY, NZ), 1.0, 6.0, ((0, 16), (2, 16))),
        "weight_one": scatter_about(key_of[1], (C2, 27 * C1), (27 * C1 // 8) ** -0.5, 0.875),
        "weight_two": scatter_about(key_of[2], (C3, 27 * C2), (27 * C2 // 8) ** -0.5, 0.625),
        "weight_three": scatter_about(key_of[3], (C4, 27 * C3), (27 * C3 // 2) ** -0.5, 0.21875),
    }


def plane_conv(planes, weight):
    height = planes.shape[2] - 2
    breadth = planes.shape[3] - 2
    shifted = [planes[a, :, b:b + height, c:c + breadth] for a in range(3) for b in range(3) for c in range(3)]
    patches = jnp.stack(shifted).reshape(27 * planes.shape[1], height * breadth)
    return jnp.dot(weight, patches, preferred_element_type=jnp.float32)


def conv_pool(padded, weight):
    out_planes = padded.shape[0] - 2
    height = padded.shape[2] - 2
    breadth = padded.shape[3] - 2

    def pair_step(plane_index):
        planes = lax.dynamic_slice_in_dim(padded, 2 * plane_index, 4, 0)
        lower_plane = jax.nn.relu(plane_conv(planes[0:3], weight))
        upper_plane = jax.nn.relu(plane_conv(planes[1:4], weight))
        summed = (lower_plane + upper_plane).reshape(weight.shape[0], height // 2, 2, breadth // 2, 2)
        return (jnp.sum(summed, axis=(2, 4)) * 0.125).astype(jnp.bfloat16)

    return lax.map(pair_step, jnp.arange(out_planes // 2, dtype=jnp.int32))


def conv_planes(padded, weight):
    out_planes = padded.shape[0] - 2

    def one_plane(plane_index):
        return plane_conv(lax.dynamic_slice_in_dim(padded, plane_index, 3, 0), weight)

    return lax.map(one_plane, jnp.arange(out_planes, dtype=jnp.int32))


def pad_all(block):
    return jnp.pad(block, ((1, 1), (0, 0), (1, 1), (1, 1)))


def reference(volume, weight_one, weight_two, weight_three):
    pooled_one = conv_pool(pad_all(volume), weight_one)
    pooled_two = conv_pool(pad_all(pooled_one), weight_two)
    result = jax.nn.relu(conv_planes(pad_all(pooled_two), weight_three))
    return jnp.moveaxis(result, 0, 1).astype(jnp.bfloat16)
```

```python
import functools

import jax
import jax.numpy as jnp
from jax import lax
from jax.experimental import pallas as pl
from jax.experimental.pallas import tpu as pltpu
from jax.sharding import PartitionSpec as P

MESH = pl.DeviceIdType.MESH
BF = jnp.bfloat16
F32 = jnp.float32
AROUND = tuple((dx, dy) for dx in (-1, 0, 1) for dy in (-1, 0, 1) if (dx, dy) != (0, 0))


def iota(shape, axis):
    return lax.broadcasted_iota(jnp.int32, shape, axis)


def choose(rows, target):
    return jnp.where(iota((rows, target.shape[1]), 0) == target, 1.0, 0.0).astype(BF)


def dot(a, b):
    return jnp.dot(a, b, preferred_element_type=F32)


def shifted(block, lane, low, high):
    zero = jnp.zeros_like(block)
    up = jnp.where(lane == low, zero, pltpu.roll(block, 1, 1))
    down = jnp.where(lane == high, zero, pltpu.roll(block, 127, 1))
    return up, down


def spread_one(w1, w1t):
    column = iota((1, 480), 1)
    c = (column >= 160).astype(jnp.int32) + (column >= 320).astype(jnp.int32)
    pos = column - 160 * c
    own = pos < 128
    y = jnp.where(own, pos & 7, jnp.where(pos < 144, -1, 8))
    i = jnp.where(own, pos >> 3, pos & 15)
    for out in range(8):
        b = y - out + 1
        target = jnp.where((b >= 0) & (b <= 2), 32 + b * 48 + c * 16 + i, -1)
        chosen = choose(176, target)
        row = (out % 2) * 128 + (out // 2) * 32
        for a, (start, skip) in enumerate(((0, 32), (128, 16), (256, 0))):
            part = dot(w1[:, start:144 * a + 144], chosen[skip:, :])
            w1t[a, row:row + 32, :] = part.astype(BF)


def spread_two(w2, w2t):
    column = iota((1, 576), 1)
    c = (column >= 192).astype(jnp.int32) + (column >= 384).astype(jnp.int32)
    pos = column - 192 * c
    group = pos >> 5
    y = jnp.where(group < 4, group, jnp.where(group == 4, -1, 4))
    i = pos & 31
    for out in range(4):
        b = y - out + 1
        target = jnp.where((b >= 0) & (b <= 2), 64 + b * 96 + c * 32 + i, -1)
        chosen = choose(352, target)
        row = (out % 2) * 128 + (out // 2) * 64
        for a, (start, skip) in enumerate(((0, 64), (256, 32), (512, 0))):
            part = dot(w2[:, start:288 * a + 288], chosen[skip:, :])
            w2t[a, row:row + 64, :] = part.astype(BF)


def spread_three(shards, w3, w3t):
    column = iota((1, 384), 1)
    c = (column >= 128).astype(jnp.int32) + (column >= 256).astype(jnp.int32)
    pos = column - 128 * c
    y = pos >> 6
    i = pos & 63
    size = 128 // shards
    for t, outs in enumerate(((0, 2), (1, -1))):
        parts = [[], [], []]
        for out in outs:
            b = y - out + 1
            target = jnp.where((b >= 0) & (b <= 2), b * 192 + c * 64 + i, -1)
            chosen = choose(576, target)
            for a in range(3):
                parts[a].append(lax.dot_general(
                    w3[a * 576:(a + 1) * 576, :], chosen, (((0,), (0,)), ((), ())),
                    preferred_element_type=F32))
        for a in range(3):
            both = jnp.stack([p.reshape(shards, size, 384) for p in parts[a]], axis=1)
            w3t[t, :, a * 384:(a + 1) * 384] = both.reshape(256, 384).astype(BF)


def kernel(groups, shards, v_hbm, w1_hbm, w2_hbm, w3_hbm, o_ref,
           p, w1, w2, w3, face, b1, w1t, q, b2e, b2o, w2t, w3t, out_s, in_s,
           load_sem, s1, r1, s2, r2, s3, r3):
    g = lax.axis_index("gx")
    s = lax.axis_index("yz")
    size = 128 // shards

    def at(dx, dy):
        return {"gx": lax.rem(g + dx + groups, groups), "yz": lax.rem(s + dy + shards, shards)}

    barrier = pltpu.get_barrier_semaphore()
    partners = [(dx, dy) for dx, dy in AROUND if dx != 0] + [(0, k) for k in range(1, shards)]
    for dx, dy in partners:
        pl.semaphore_signal(barrier, inc=1, device_id=at(dx, dy), device_id_type=MESH)

    loads = [
        pltpu.make_async_copy(v_hbm, p.at[1:9, 0:128], load_sem.at[0]),
        pltpu.make_async_copy(w1_hbm, w1, load_sem.at[1]),
        pltpu.make_async_copy(w2_hbm, w2, load_sem.at[2]),
        pltpu.make_async_copy(w3_hbm, w3, load_sem.at[3]),
    ]
    for load in loads:
        load.start()

    loads[0].wait()
    which = iota((32, 128), 0)
    ends = jnp.where(iota((32, 128), 1) == (which & 15) * 8 + (which >> 4) * 7, 1.0, 0.0).astype(BF)
    for x in range(0, 8, 2):
        cells = dot(ends, jnp.concatenate([p[1 + x, 0:128, :], p[2 + x, 0:128, :]], axis=1)).astype(BF)
        for k in range(2):
            face[0, x + k] = cells[0:16, k * 128:(k + 1) * 128]
            face[1, x + k] = cells[16:32, k * 128:(k + 1) * 128]

    pl.semaphore_wait(barrier, len(partners))

    first = []
    for k, (dx, dy) in enumerate(AROUND):
        plane = 7 if dx > 0 else 0
        to = 0 if dx > 0 else 9
        side = 1 if dy > 0 else 0
        rows = slice(128, 144) if dy > 0 else slice(144, 160)
        if dy == 0:
            src, dst = p.at[1 + plane, 0:128], p.at[to, 0:128]
        elif dx == 0:
            src, dst = face.at[side], p.at[1:9, rows]
        else:
            src, dst = face.at[side, plane], p.at[to, rows]
        first.append(pltpu.make_async_remote_copy(
            src_ref=src, dst_ref=dst, send_sem=s1.at[k], recv_sem=r1.at[k],
            device_id=at(dx, dy), device_id_type=MESH))
    for copy in first:
        copy.start()

    loads[1].wait()
    spread_one(w1, w1t)
    loads[2].wait()
    spread_two(w2, w2t)

    for copy in first:
        copy.wait_recv()

    @pl.when(g == 0)
    def _():
        p[0] = jnp.zeros((160, 128), BF)

    @pl.when(g == groups - 1)
    def _():
        p[9] = jnp.zeros((160, 128), BF)

    @pl.when(s == 0)
    def _():
        p[:, 128:144, :] = jnp.zeros((10, 16, 128), BF)

    @pl.when(s == shards - 1)
    def _():
        p[:, 144:160, :] = jnp.zeros((10, 16, 128), BF)

    lane = iota((160, 128), 1)
    for x in range(10):
        mid = p[x]
        up, down = shifted(mid, lane, 0, 127)
        b1[x, 0:160] = up
        b1[x, 160:320] = mid
        b1[x, 320:480] = down
    pooled = []
    for x in range(0, 8, 2):
        total = None
        for a in range(3):
            part = dot(w1t[a], jnp.concatenate([b1[x + a], b1[x + a + 1]], axis=1))
            total = part if total is None else total + part
        total = jnp.maximum(total, 0.0)
        total = total[0:128] + total[128:256]
        total = total[:, 0:128] + total[:, 128:256]
        total = (total + pltpu.roll(total, 127, 1)) * 0.125
        pooled.append(total.astype(BF))
    lanes = iota((256, 128), 1)
    pick = jnp.where(iota((256, 128), 0) == (lanes >> 6) * 128 + (lanes & 63) * 2, 1.0, 0.0).astype(BF)
    for j in range(2):
        q[2 + j, 0:128, :] = dot(jnp.concatenate(pooled[2 * j:2 * j + 2], axis=1), pick).astype(BF)

    second = []
    for k, (dx, dy) in enumerate(AROUND):
        to = slice(2, 4) if dx == 0 else (slice(0, 2) if dx > 0 else slice(4, 6))
        if dy == 0:
            rows, into = slice(0, 128), slice(0, 128)
        elif dy > 0:
            rows, into = slice(96, 128), slice(128, 160)
        else:
            rows, into = slice(0, 32), slice(160, 192)
        second.append(pltpu.make_async_remote_copy(
            src_ref=q.at[2:4, rows], dst_ref=q.at[to, into], send_sem=s2.at[k], recv_sem=r2.at[k],
            device_id=at(dx, dy), device_id_type=MESH))
    for copy in second:
        copy.start()

    loads[3].wait()
    spread_three(shards, w3, w3t)

    for copy in second:
        copy.wait_recv()

    @pl.when(g == 0)
    def _():
        q[0:2] = jnp.zeros((2, 192, 128), BF)

    @pl.when(g == groups - 1)
    def _():
        q[4:6] = jnp.zeros((2, 192, 128), BF)

    @pl.when(s == 0)
    def _():
        q[:, 128:160, :] = jnp.zeros((6, 32, 128), BF)

    @pl.when(s == shards - 1)
    def _():
        q[:, 160:192, :] = jnp.zeros((6, 32, 128), BF)

    lane = iota((192, 128), 1) & 63
    half = iota((192, 128), 1) < 64
    for j in range(5):
        if j > 0:
            mid = q[j]
            up, down = shifted(mid, lane, 0, 63)
            b2e[j - 1, 0:192] = up
            b2e[j - 1, 192:384] = mid
            b2e[j - 1, 384:576] = down
        mid = jnp.where(half, pltpu.roll(q[j], 64, 1), pltpu.roll(q[j + 1], 64, 1))
        up, down = shifted(mid, lane, 0, 63)
        b2o[j, 0:192] = up
        b2o[j, 192:384] = mid
        b2o[j, 384:576] = down
    pooled = []
    for j in range(0, 4, 2):
        total = dot(w2t[0], jnp.concatenate([b2o[j], b2o[j + 1]], axis=1))
        total += dot(w2t[1], jnp.concatenate([b2e[j], b2e[j + 1]], axis=1))
        total += dot(w2t[2], jnp.concatenate([b2o[j + 1], b2o[j + 2]], axis=1))
        total = jnp.maximum(total, 0.0)
        total = total[0:128] + total[128:256]
        for k in range(2):
            pair = total[:, k * 128:(k + 1) * 128]
            pair = pair + pltpu.roll(pair, 64, 1)
            pair = (pair + pltpu.roll(pair, 127, 1)) * 0.125
            if j + k == 0:
                pair = jnp.where(g == 0, 0.0, pair)
            if j + k == 3:
                pair = jnp.where(g == groups - 1, 0.0, pair)
            pooled.append(pair)

    low = iota((128, 128), 1) < 64
    stacked = jnp.concatenate(
        [jnp.where(low, pooled[a], pooled[a + 1]).astype(BF) for a in range(3)], axis=0)
    column = iota((1, 384), 1)
    c = column >> 7
    inside = column & 127
    z = (inside & 31) + c - 1
    target = jnp.where((z >= 0) & (z < 32), (inside >> 6) * 64 + 2 * z, -1)
    planes = dot(stacked, choose(128, target)).astype(BF)
    right = jnp.concatenate(
        [planes[a * 128:(a + 1) * 128, c * 128:(c + 1) * 128] for a in range(3) for c in range(3)], axis=0)
    even = dot(w3t[0], right)
    odd = dot(w3t[1], right)
    parity = (iota((256, 128), 1) & 32) == 0
    out_s[...] = jnp.where(parity, even, odd).astype(BF).reshape(shards, 2 * size, 128)

    third = []
    for k in range(1, shards):
        there = at(0, k)
        third.append(pltpu.make_async_remote_copy(
            src_ref=out_s.at[there["yz"]], dst_ref=in_s.at[s], send_sem=s3.at[k], recv_sem=r3.at[k],
            device_id=there, device_id_type=MESH))
    for copy in third:
        copy.start()
    in_s[s] = out_s[s]
    for copy in first + second:
        copy.wait_send()
    for copy in third:
        copy.wait_recv()

    low = iota((size, 128), 1) < 64
    parity = (iota((size, 128), 1) & 32) == 0
    done = []
    for n in range(shards):
        below = in_s[n - 1, size:, :].astype(F32) if n > 0 else jnp.zeros((size, 128), F32)
        above = in_s[n + 1, size:, :].astype(F32) if n < shards - 1 else jnp.zeros((size, 128), F32)
        whole = in_s[n, 0:size, :].astype(F32) + jnp.where(parity, below, above)
        done.append(jnp.maximum(whole, 0.0))
    for n in range(0, shards, 2):
        at0 = jnp.where(low, done[n], pltpu.roll(done[n + 1], 64, 1))
        at1 = jnp.where(low, pltpu.roll(done[n], 64, 1), done[n + 1])
        o_ref[0, :, n * 64:n * 64 + 128] = at0.astype(BF)
        o_ref[1, :, n * 64:n * 64 + 128] = at1.astype(BF)
    for copy in third:
        copy.wait_send()


def per_device(volume, weight_one, weight_two, weight_three):
    groups, shards = lax.axis_size("gx"), lax.axis_size("yz")
    size = 128 // shards
    anywhere = pl.BlockSpec(memory_space=pl.ANY)
    dma = pltpu.SemaphoreType.DMA
    out = pl.pallas_call(
        functools.partial(kernel, groups, shards),
        out_shape=jax.ShapeDtypeStruct((2, size, shards * 64), BF),
        in_specs=[anywhere] * 4,
        out_specs=pl.BlockSpec(memory_space=pltpu.VMEM),
        scratch_shapes=[
            pltpu.VMEM((10, 160, 128), BF),
            pltpu.VMEM((32, 432), BF),
            pltpu.VMEM((64, 864), BF),
            pltpu.VMEM((1728, 128), BF),
            pltpu.VMEM((2, 8, 16, 128), BF),
            pltpu.VMEM((10, 480, 128), BF),
            pltpu.VMEM((3, 256, 480), BF),
            pltpu.VMEM((6, 192, 128), BF),
            pltpu.VMEM((4, 576, 128), BF),
            pltpu.VMEM((5, 576, 128), BF),
            pltpu.VMEM((3, 256, 576), BF),
            pltpu.VMEM((2, 256, 1152), BF),
            pltpu.VMEM((shards, 2 * size, 128), BF),
            pltpu.VMEM((shards, 2 * size, 128), BF),
            dma((4,)),
            dma((8,)), dma((8,)), dma((8,)), dma((8,)),
            dma((shards,)), dma((shards,)),
        ],
        compiler_params=pltpu.CompilerParams(collective_id=0, has_side_effects=True),
    )(volume.reshape(8, 128, 128), weight_one, weight_two, weight_three.T)
    return jnp.moveaxis(out, 0, 1)


def solution(mesh):
    placed = (P("gx", None, "yz", None), P(), P(), P())
    return jax.shard_map(
        per_device, mesh=mesh, in_specs=placed, out_specs=P("yz", "gx", None), check_vma=False
    )
```

```python
import functools

import jax
import jax.numpy as jnp
from jax import lax
from jax.experimental import pallas as pl
from jax.experimental.pallas import tpu as pltpu
from jax.sharding import PartitionSpec as P

MESH = pl.DeviceIdType.MESH
BF = jnp.bfloat16
F32 = jnp.float32
AROUND = tuple((dx, dy) for dx in (-1, 0, 1) for dy in (-1, 0, 1) if (dx, dy) != (0, 0))


def iota(shape, axis):
    return lax.broadcasted_iota(jnp.int32, shape, axis)


def start(copy):
    copy.start()


def receive(copy):
    copy.wait_recv()


def sent(copy):
    copy.wait_send()


def choose(rows, target):
    return jnp.where(iota((rows, target.shape[1]), 0) == target, 1.0, 0.0).astype(BF)


def dot(a, b):
    return jnp.dot(a, b, preferred_element_type=F32)


def shifted(block, lane, low, high):
    zero = jnp.zeros_like(block)
    up = jnp.where(lane == low, zero, pltpu.roll(block, 1, 1))
    down = jnp.where(lane == high, zero, pltpu.roll(block, 127, 1))
    return up, down


def spread_one(w1, w1t):
    column = iota((1, 480), 1)
    c = (column >= 160).astype(jnp.int32) + (column >= 320).astype(jnp.int32)
    pos = column - 160 * c
    own = pos < 128
    y = jnp.where(own, pos & 7, jnp.where(pos < 144, -1, 8))
    i = jnp.where(own, pos >> 3, pos & 15)
    for out in range(8):
        b = y - out + 1
        target = jnp.where((b >= 0) & (b <= 2), 32 + b * 48 + c * 16 + i, -1)
        chosen = choose(176, target)
        row = (out % 2) * 128 + (out // 2) * 32
        for a, (start, skip) in enumerate(((0, 32), (128, 16), (256, 0))):
            part = dot(w1[:, start:144 * a + 144], chosen[skip:, :])
            w1t[a, row:row + 32, :] = part.astype(BF)


def spread_two(w2, w2t):
    column = iota((1, 576), 1)
    c = (column >= 192).astype(jnp.int32) + (column >= 384).astype(jnp.int32)
    pos = column - 192 * c
    group = pos >> 5
    y = jnp.where(group < 4, group, jnp.where(group == 4, -1, 4))
    i = pos & 31
    for out in range(4):
        b = y - out + 1
        target = jnp.where((b >= 0) & (b <= 2), 64 + b * 96 + c * 32 + i, -1)
        chosen = choose(352, target)
        row = (out % 2) * 128 + (out // 2) * 64
        for a, (start, skip) in enumerate(((0, 64), (256, 32), (512, 0))):
            part = dot(w2[:, start:288 * a + 288], chosen[skip:, :])
            w2t[a, row:row + 64, :] = part.astype(BF)


def spread_three(shards, w3, w3t):
    column = iota((1, 384), 1)
    c = (column >= 128).astype(jnp.int32) + (column >= 256).astype(jnp.int32)
    pos = column - 128 * c
    y = pos >> 6
    i = pos & 63
    size = 128 // shards
    for t, outs in enumerate(((0, 2), (1, -1))):
        parts = [[], [], []]
        for out in outs:
            b = y - out + 1
            target = jnp.where((b >= 0) & (b <= 2), b * 192 + c * 64 + i, -1)
            chosen = choose(576, target)
            for a in range(3):
                parts[a].append(lax.dot_general(
                    w3[a * 576:(a + 1) * 576, :], chosen, (((0,), (0,)), ((), ())),
                    preferred_element_type=F32))
        for a in range(3):
            both = jnp.stack([p.reshape(shards, size, 384) for p in parts[a]], axis=1)
            w3t[t, :, a * 384:(a + 1) * 384] = both.reshape(256, 384).astype(BF)


def kernel(groups, shards, v_hbm, w1_hbm, w2_hbm, w3_hbm, o_ref,
           p, w1, w2, w3, face, b1, w1t, q, b2e, b2o, w2t, w3t, out_s, in_s,
           load_sem, s1, r1, s2, r2, s3, r3):
    g = lax.axis_index("gx")
    s = lax.axis_index("yz")
    size = 128 // shards

    def at(dx, dy):
        return {"gx": lax.rem(g + dx + groups, groups), "yz": lax.rem(s + dy + shards, shards)}

    def has(dx, dy):
        x = {-1: g > 0, 0: None, 1: g < groups - 1}[dx]
        y = {-1: s > 0, 0: None, 1: s < shards - 1}[dy]
        return y if x is None else (x if y is None else x & y)

    def each(copies, act, sign):
        for (dx, dy), copy in zip(AROUND, copies):
            pl.when(has(sign * dx, sign * dy))(functools.partial(act, copy))

    barrier = pltpu.get_barrier_semaphore()
    count = shards - 1
    for dx, dy in AROUND:
        if dx != 0:
            there = has(dx, dy)
            count = count + there.astype(jnp.int32)
            pl.when(there)(functools.partial(
                pl.semaphore_signal, barrier, inc=1, device_id=at(dx, dy), device_id_type=MESH))
    for k in range(1, shards):
        pl.semaphore_signal(barrier, inc=1, device_id=at(0, k), device_id_type=MESH)

    loads = [
        pltpu.make_async_copy(v_hbm, p.at[1:9, 0:128], load_sem.at[0]),
        pltpu.make_async_copy(w1_hbm, w1, load_sem.at[1]),
        pltpu.make_async_copy(w2_hbm, w2, load_sem.at[2]),
        pltpu.make_async_copy(w3_hbm, w3, load_sem.at[3]),
    ]
    for load in loads:
        load.start()

    loads[0].wait()
    which = iota((32, 128), 0)
    ends = jnp.where(iota((32, 128), 1) == (which & 15) * 8 + (which >> 4) * 7, 1.0, 0.0).astype(BF)
    for x in range(0, 8, 2):
        cells = dot(ends, jnp.concatenate([p[1 + x, 0:128, :], p[2 + x, 0:128, :]], axis=1)).astype(BF)
        for k in range(2):
            face[0, x + k] = cells[0:16, k * 128:(k + 1) * 128]
            face[1, x + k] = cells[16:32, k * 128:(k + 1) * 128]

    @pl.when(g == 0)
    def _():
        p[0] = jnp.zeros((160, 128), BF)
        q[0:2] = jnp.zeros((2, 192, 128), BF)

    @pl.when(g == groups - 1)
    def _():
        p[9] = jnp.zeros((160, 128), BF)
        q[4:6] = jnp.zeros((2, 192, 128), BF)

    @pl.when(s == 0)
    def _():
        p[:, 128:144, :] = jnp.zeros((10, 16, 128), BF)
        q[:, 128:160, :] = jnp.zeros((6, 32, 128), BF)

    @pl.when(s == shards - 1)
    def _():
        p[:, 144:160, :] = jnp.zeros((10, 16, 128), BF)
        q[:, 160:192, :] = jnp.zeros((6, 32, 128), BF)

    pl.semaphore_wait(barrier, count)

    first = []
    for k, (dx, dy) in enumerate(AROUND):
        plane = 7 if dx > 0 else 0
        to = 0 if dx > 0 else 9
        side = 1 if dy > 0 else 0
        rows = slice(128, 144) if dy > 0 else slice(144, 160)
        if dy == 0:
            src, dst = p.at[1 + plane, 0:128], p.at[to, 0:128]
        elif dx == 0:
            src, dst = face.at[side], p.at[1:9, rows]
        else:
            src, dst = face.at[side, plane], p.at[to, rows]
        first.append(pltpu.make_async_remote_copy(
            src_ref=src, dst_ref=dst, send_sem=s1.at[k], recv_sem=r1.at[k],
            device_id=at(dx, dy), device_id_type=MESH))
    each(first, start, 1)

    loads[1].wait()
    spread_one(w1, w1t)
    loads[2].wait()
    spread_two(w2, w2t)

    each(first, receive, -1)

    lane = iota((160, 128), 1)
    for x in range(10):
        mid = p[x]
        up, down = shifted(mid, lane, 0, 127)
        b1[x, 0:160] = up
        b1[x, 160:320] = mid
        b1[x, 320:480] = down
    pooled = []
    for x in range(0, 8, 2):
        total = None
        for a in range(3):
            part = dot(w1t[a], jnp.concatenate([b1[x + a], b1[x + a + 1]], axis=1))
            total = part if total is None else total + part
        total = jnp.maximum(total, 0.0)
        total = total[0:128] + total[128:256]
        total = total[:, 0:128] + total[:, 128:256]
        total = (total + pltpu.roll(total, 127, 1)) * 0.125
        pooled.append(total.astype(BF))
    lanes = iota((256, 128), 1)
    pick = jnp.where(iota((256, 128), 0) == (lanes >> 6) * 128 + (lanes & 63) * 2, 1.0, 0.0).astype(BF)
    for j in range(2):
        q[2 + j, 0:128, :] = dot(jnp.concatenate(pooled[2 * j:2 * j + 2], axis=1), pick).astype(BF)

    second = []
    for k, (dx, dy) in enumerate(AROUND):
        to = slice(2, 4) if dx == 0 else (slice(0, 2) if dx > 0 else slice(4, 6))
        if dy == 0:
            rows, into = slice(0, 128), slice(0, 128)
        elif dy > 0:
            rows, into = slice(96, 128), slice(128, 160)
        else:
            rows, into = slice(0, 32), slice(160, 192)
        second.append(pltpu.make_async_remote_copy(
            src_ref=q.at[2:4, rows], dst_ref=q.at[to, into], send_sem=s2.at[k], recv_sem=r2.at[k],
            device_id=at(dx, dy), device_id_type=MESH))
    each(second, start, 1)

    loads[3].wait()
    spread_three(shards, w3, w3t)

    each(second, receive, -1)

    lane = iota((192, 128), 1) & 63
    half = iota((192, 128), 1) < 64
    for j in range(5):
        if j > 0:
            mid = q[j]
            up, down = shifted(mid, lane, 0, 63)
            b2e[j - 1, 0:192] = up
            b2e[j - 1, 192:384] = mid
            b2e[j - 1, 384:576] = down
        mid = jnp.where(half, pltpu.roll(q[j], 64, 1), pltpu.roll(q[j + 1], 64, 1))
        up, down = shifted(mid, lane, 0, 63)
        b2o[j, 0:192] = up
        b2o[j, 192:384] = mid
        b2o[j, 384:576] = down
    pooled = []
    for j in range(0, 4, 2):
        total = dot(w2t[0], jnp.concatenate([b2o[j], b2o[j + 1]], axis=1))
        total += dot(w2t[1], jnp.concatenate([b2e[j], b2e[j + 1]], axis=1))
        total += dot(w2t[2], jnp.concatenate([b2o[j + 1], b2o[j + 2]], axis=1))
        total = jnp.maximum(total, 0.0)
        total = total[0:128] + total[128:256]
        for k in range(2):
            pair = total[:, k * 128:(k + 1) * 128]
            pair = pair + pltpu.roll(pair, 64, 1)
            pair = (pair + pltpu.roll(pair, 127, 1)) * 0.125
            if j + k == 0:
                pair = jnp.where(g == 0, 0.0, pair)
            if j + k == 3:
                pair = jnp.where(g == groups - 1, 0.0, pair)
            pooled.append(pair)

    low = iota((128, 128), 1) < 64
    stacked = jnp.concatenate(
        [jnp.where(low, pooled[a], pooled[a + 1]).astype(BF) for a in range(3)], axis=0)
    column = iota((1, 384), 1)
    c = column >> 7
    inside = column & 127
    z = (inside & 31) + c - 1
    target = jnp.where((z >= 0) & (z < 32), (inside >> 6) * 64 + 2 * z, -1)
    planes = dot(stacked, choose(128, target)).astype(BF)
    right = jnp.concatenate(
        [planes[a * 128:(a + 1) * 128, c * 128:(c + 1) * 128] for a in range(3) for c in range(3)], axis=0)
    even = dot(w3t[0], right)
    odd = dot(w3t[1], right)
    parity = (iota((256, 128), 1) & 32) == 0
    out_s[...] = jnp.where(parity, even, odd).astype(BF).reshape(shards, 2 * size, 128)

    third = []
    for k in range(1, shards):
        there = at(0, k)
        third.append(pltpu.make_async_remote_copy(
            src_ref=out_s.at[there["yz"]], dst_ref=in_s.at[s], send_sem=s3.at[k], recv_sem=r3.at[s],
            device_id=there, device_id_type=MESH))
    for copy in third:
        copy.start()
    in_s[s] = out_s[s]
    each(first, sent, 1)
    each(second, sent, 1)

    low = iota((size, 128), 1) < 64
    parity = (iota((size, 128), 1) & 32) == 0
    nothing = jnp.zeros((size, 128), F32)
    main, cross = [], [nothing]
    for n in range(shards + 1):
        if n < shards:
            @pl.when(n != s)
            def _():
                pltpu.make_async_remote_copy(
                    src_ref=out_s.at[0], dst_ref=in_s.at[n], send_sem=s3.at[0], recv_sem=r3.at[n],
                    device_id=at(0, 1), device_id_type=MESH).wait_recv()
            block = in_s[n].astype(F32)
            main.append(block[0:size])
            cross.append(block[size:])
        else:
            cross.append(nothing)
        if n >= 2 and n % 2 == 0:
            left, right = [
                jnp.maximum(main[m] + jnp.where(parity, cross[m], cross[m + 2]), 0.0) for m in (n - 2, n - 1)]
            lanes = slice(n * 64 - 128, n * 64)
            o_ref[0, :, lanes] = jnp.where(low, left, pltpu.roll(right, 64, 1)).astype(BF)
            o_ref[1, :, lanes] = jnp.where(low, pltpu.roll(left, 64, 1), right).astype(BF)
    for copy in third:
        copy.wait_send()


def per_device(volume, weight_one, weight_two, weight_three):
    groups, shards = lax.axis_size("gx"), lax.axis_size("yz")
    size = 128 // shards
    anywhere = pl.BlockSpec(memory_space=pl.ANY)
    dma = pltpu.SemaphoreType.DMA
    out = pl.pallas_call(
        functools.partial(kernel, groups, shards),
        out_shape=jax.ShapeDtypeStruct((2, size, shards * 64), BF),
        in_specs=[anywhere] * 4,
        out_specs=pl.BlockSpec(memory_space=pltpu.VMEM),
        scratch_shapes=[
            pltpu.VMEM((10, 160, 128), BF),
            pltpu.VMEM((32, 432), BF),
            pltpu.VMEM((64, 864), BF),
            pltpu.VMEM((1728, 128), BF),
            pltpu.VMEM((2, 8, 16, 128), BF),
            pltpu.VMEM((10, 480, 128), BF),
            pltpu.VMEM((3, 256, 480), BF),
            pltpu.VMEM((6, 192, 128), BF),
            pltpu.VMEM((4, 576, 128), BF),
            pltpu.VMEM((5, 576, 128), BF),
            pltpu.VMEM((3, 256, 576), BF),
            pltpu.VMEM((2, 256, 1152), BF),
            pltpu.VMEM((shards, 2 * size, 128), BF),
            pltpu.VMEM((shards, 2 * size, 128), BF),
            dma((4,)),
            dma((8,)), dma((8,)), dma((8,)), dma((8,)),
            dma((shards,)), dma((shards,)),
        ],
        compiler_params=pltpu.CompilerParams(collective_id=0, has_side_effects=True),
    )(volume.reshape(8, 128, 128), weight_one, weight_two, weight_three.T)
    return jnp.moveaxis(out, 0, 1)


def solution(mesh):
    placed = (P("gx", None, "yz", None), P(), P(), P())
    return jax.shard_map(
        per_device, mesh=mesh, in_specs=placed, out_specs=P("yz", "gx", None), check_vma=False
    )
```

```python
import functools

import jax
import jax.numpy as jnp
from jax import lax
from jax.experimental import pallas as pl
from jax.experimental.pallas import tpu as pltpu
from jax.sharding import PartitionSpec as P

MESH = pl.DeviceIdType.MESH
BF = jnp.bfloat16
F32 = jnp.float32
AROUND = tuple((dx, dy) for dx in (-1, 0, 1) for dy in (-1, 0, 1) if (dx, dy) != (0, 0))


def iota(shape, axis):
    return lax.broadcasted_iota(jnp.int32, shape, axis)


def start(copy):
    copy.start()


def receive(copy):
    copy.wait_recv()


def sent(copy):
    copy.wait_send()


def choose(rows, target):
    return jnp.where(iota((rows, target.shape[1]), 0) == target, 1.0, 0.0).astype(BF)


def dot(a, b):
    return jnp.dot(a, b, preferred_element_type=F32)


def shifted(block, lane, low, high):
    zero = jnp.zeros_like(block)
    up = jnp.where(lane == low, zero, pltpu.roll(block, 1, 1))
    down = jnp.where(lane == high, zero, pltpu.roll(block, 127, 1))
    return up, down


def spread_one(w1, w1t):
    column = iota((1, 480), 1)
    c = (column >= 160).astype(jnp.int32) + (column >= 320).astype(jnp.int32)
    pos = column - 160 * c
    own = pos < 128
    y = jnp.where(own, pos & 7, jnp.where(pos < 144, -1, 8))
    i = jnp.where(own, pos >> 3, pos & 15)
    for out in range(8):
        b = y - out + 1
        target = jnp.where((b >= 0) & (b <= 2), 32 + b * 48 + c * 16 + i, -1)
        chosen = choose(176, target)
        row = (out % 2) * 128 + (out // 2) * 32
        for a, (start, skip) in enumerate(((0, 32), (128, 16), (256, 0))):
            part = dot(w1[:, start:144 * a + 144], chosen[skip:, :])
            w1t[a, row:row + 32, :] = part.astype(BF)


def spread_two(w2, w2t):
    column = iota((1, 576), 1)
    c = (column >= 192).astype(jnp.int32) + (column >= 384).astype(jnp.int32)
    pos = column - 192 * c
    group = pos >> 5
    y = jnp.where(group < 4, group, jnp.where(group == 4, -1, 4))
    i = pos & 31
    for out in range(4):
        b = y - out + 1
        target = jnp.where((b >= 0) & (b <= 2), 64 + b * 96 + c * 32 + i, -1)
        chosen = choose(352, target)
        row = (out % 2) * 128 + (out // 2) * 64
        for a, (start, skip) in enumerate(((0, 64), (256, 32), (512, 0))):
            part = dot(w2[:, start:288 * a + 288], chosen[skip:, :])
            w2t[a, row:row + 64, :] = part.astype(BF)


def spread_three(shards, w3, w3t):
    column = iota((1, 384), 1)
    c = (column >= 128).astype(jnp.int32) + (column >= 256).astype(jnp.int32)
    pos = column - 128 * c
    y = pos >> 6
    i = pos & 63
    size = 128 // shards
    for t, outs in enumerate(((0, 2), (1, -1))):
        parts = [[], [], []]
        for out in outs:
            b = y - out + 1
            target = jnp.where((b >= 0) & (b <= 2), b * 192 + c * 64 + i, -1)
            chosen = choose(576, target)
            for a in range(3):
                parts[a].append(lax.dot_general(
                    w3[a * 576:(a + 1) * 576, :], chosen, (((0,), (0,)), ((), ())),
                    preferred_element_type=F32))
        for a in range(3):
            both = jnp.stack([p.reshape(shards, size, 384) for p in parts[a]], axis=1)
            w3t[t, :, a * 384:(a + 1) * 384] = both.reshape(256, 384).astype(BF)


def kernel(groups, shards, v_hbm, w1_hbm, w2_hbm, w3_hbm, o_ref,
           p, w1, w2, w3, face, b1, w1t, q, b2e, b2o, w2t, w3t, out_s, in_s,
           load_sem, s1, r1, s2, r2, s3, r3, known):
    g = lax.axis_index("gx")
    s = lax.axis_index("yz")
    size = 128 // shards

    def at(dx, dy):
        return {"gx": lax.rem(g + dx + groups, groups), "yz": lax.rem(s + dy + shards, shards)}

    def has(dx, dy):
        x = {-1: g > 0, 0: None, 1: g < groups - 1}[dx]
        y = {-1: s > 0, 0: None, 1: s < shards - 1}[dy]
        return y if x is None else (x if y is None else x & y)

    def each(copies, act, sign):
        for (dx, dy), copy in zip(AROUND, copies):
            pl.when(has(sign * dx, sign * dy))(functools.partial(act, copy))

    barrier = pltpu.get_barrier_semaphore()
    count = 0
    for dx, dy in AROUND:
        there = has(dx, dy)
        count = count + there.astype(jnp.int32)
        pl.when(there)(functools.partial(
            pl.semaphore_signal, barrier, inc=1, device_id=at(dx, dy), device_id_type=MESH))

    rounds = []
    while 2 << len(rounds) < shards:
        rounds.append(2 << len(rounds))

    def tell(r):
        for side, d in enumerate((-rounds[r], rounds[r])):
            pl.when((s + d >= 0) & (s + d < shards))(functools.partial(
                pl.semaphore_signal, known.at[r, side], inc=1,
                device_id={"gx": g, "yz": lax.rem(s + d + shards, shards)}, device_id_type=MESH))

    def hear(r):
        for side, d in enumerate((rounds[r], -rounds[r])):
            pl.when((s + d >= 0) & (s + d < shards))(functools.partial(
                pl.semaphore_wait, known.at[r, side], 1))

    loads = [
        pltpu.make_async_copy(v_hbm, p.at[1:9, 0:128], load_sem.at[0]),
        pltpu.make_async_copy(w1_hbm, w1, load_sem.at[1]),
        pltpu.make_async_copy(w2_hbm, w2, load_sem.at[2]),
        pltpu.make_async_copy(w3_hbm, w3, load_sem.at[3]),
    ]
    for load in loads:
        load.start()

    loads[0].wait()
    which = iota((32, 128), 0)
    ends = jnp.where(iota((32, 128), 1) == (which & 15) * 8 + (which >> 4) * 7, 1.0, 0.0).astype(BF)
    for x in range(0, 8, 2):
        cells = dot(ends, jnp.concatenate([p[1 + x, 0:128, :], p[2 + x, 0:128, :]], axis=1)).astype(BF)
        for k in range(2):
            face[0, x + k] = cells[0:16, k * 128:(k + 1) * 128]
            face[1, x + k] = cells[16:32, k * 128:(k + 1) * 128]

    @pl.when(g == 0)
    def _():
        p[0] = jnp.zeros((160, 128), BF)
        q[0:2] = jnp.zeros((2, 192, 128), BF)

    @pl.when(g == groups - 1)
    def _():
        p[9] = jnp.zeros((160, 128), BF)
        q[4:6] = jnp.zeros((2, 192, 128), BF)

    @pl.when(s == 0)
    def _():
        p[:, 128:144, :] = jnp.zeros((10, 16, 128), BF)
        q[:, 128:160, :] = jnp.zeros((6, 32, 128), BF)

    @pl.when(s == shards - 1)
    def _():
        p[:, 144:160, :] = jnp.zeros((10, 16, 128), BF)
        q[:, 160:192, :] = jnp.zeros((6, 32, 128), BF)

    pl.semaphore_wait(barrier, count)

    first = []
    for k, (dx, dy) in enumerate(AROUND):
        plane = 7 if dx > 0 else 0
        to = 0 if dx > 0 else 9
        side = 1 if dy > 0 else 0
        rows = slice(128, 144) if dy > 0 else slice(144, 160)
        if dy == 0:
            src, dst = p.at[1 + plane, 0:128], p.at[to, 0:128]
        elif dx == 0:
            src, dst = face.at[side], p.at[1:9, rows]
        else:
            src, dst = face.at[side, plane], p.at[to, rows]
        first.append(pltpu.make_async_remote_copy(
            src_ref=src, dst_ref=dst, send_sem=s1.at[k], recv_sem=r1.at[k],
            device_id=at(dx, dy), device_id_type=MESH))
    each(first, start, 1)

    loads[1].wait()
    spread_one(w1, w1t)
    loads[2].wait()
    spread_two(w2, w2t)

    each(first, receive, -1)
    tell(0)

    lane = iota((160, 128), 1)
    for x in range(10):
        mid = p[x]
        up, down = shifted(mid, lane, 0, 127)
        b1[x, 0:160] = up
        b1[x, 160:320] = mid
        b1[x, 320:480] = down
    pooled = []
    for x in range(0, 8, 2):
        total = None
        for a in range(3):
            part = dot(w1t[a], jnp.concatenate([b1[x + a], b1[x + a + 1]], axis=1))
            total = part if total is None else total + part
        total = jnp.maximum(total, 0.0)
        total = total[0:128] + total[128:256]
        total = total[:, 0:128] + total[:, 128:256]
        total = (total + pltpu.roll(total, 127, 1)) * 0.125
        pooled.append(total.astype(BF))
    lanes = iota((256, 128), 1)
    pick = jnp.where(iota((256, 128), 0) == (lanes >> 6) * 128 + (lanes & 63) * 2, 1.0, 0.0).astype(BF)
    for j in range(2):
        q[2 + j, 0:128, :] = dot(jnp.concatenate(pooled[2 * j:2 * j + 2], axis=1), pick).astype(BF)

    second = []
    for k, (dx, dy) in enumerate(AROUND):
        to = slice(2, 4) if dx == 0 else (slice(0, 2) if dx > 0 else slice(4, 6))
        if dy == 0:
            rows, into = slice(0, 128), slice(0, 128)
        elif dy > 0:
            rows, into = slice(96, 128), slice(128, 160)
        else:
            rows, into = slice(0, 32), slice(160, 192)
        second.append(pltpu.make_async_remote_copy(
            src_ref=q.at[2:4, rows], dst_ref=q.at[to, into], send_sem=s2.at[k], recv_sem=r2.at[k],
            device_id=at(dx, dy), device_id_type=MESH))
    each(second, start, 1)

    loads[3].wait()
    spread_three(shards, w3, w3t)

    for r in range(len(rounds) - 1):
        hear(r)
        tell(r + 1)
    each(second, receive, -1)

    lane = iota((192, 128), 1) & 63
    half = iota((192, 128), 1) < 64
    for j in range(5):
        if j > 0:
            mid = q[j]
            up, down = shifted(mid, lane, 0, 63)
            b2e[j - 1, 0:192] = up
            b2e[j - 1, 192:384] = mid
            b2e[j - 1, 384:576] = down
        mid = jnp.where(half, pltpu.roll(q[j], 64, 1), pltpu.roll(q[j + 1], 64, 1))
        up, down = shifted(mid, lane, 0, 63)
        b2o[j, 0:192] = up
        b2o[j, 192:384] = mid
        b2o[j, 384:576] = down
    pooled = []
    for j in range(0, 4, 2):
        total = dot(w2t[0], jnp.concatenate([b2o[j], b2o[j + 1]], axis=1))
        total += dot(w2t[1], jnp.concatenate([b2e[j], b2e[j + 1]], axis=1))
        total += dot(w2t[2], jnp.concatenate([b2o[j + 1], b2o[j + 2]], axis=1))
        total = jnp.maximum(total, 0.0)
        total = total[0:128] + total[128:256]
        for k in range(2):
            pair = total[:, k * 128:(k + 1) * 128]
            pair = pair + pltpu.roll(pair, 64, 1)
            pair = (pair + pltpu.roll(pair, 127, 1)) * 0.125
            if j + k == 0:
                pair = jnp.where(g == 0, 0.0, pair)
            if j + k == 3:
                pair = jnp.where(g == groups - 1, 0.0, pair)
            pooled.append(pair)

    low = iota((128, 128), 1) < 64
    stacked = jnp.concatenate(
        [jnp.where(low, pooled[a], pooled[a + 1]).astype(BF) for a in range(3)], axis=0)
    column = iota((1, 384), 1)
    c = column >> 7
    inside = column & 127
    z = (inside & 31) + c - 1
    target = jnp.where((z >= 0) & (z < 32), (inside >> 6) * 64 + 2 * z, -1)
    planes = dot(stacked, choose(128, target)).astype(BF)
    right = jnp.concatenate(
        [planes[a * 128:(a + 1) * 128, c * 128:(c + 1) * 128] for a in range(3) for c in range(3)], axis=0)
    even = dot(w3t[0], right)
    odd = dot(w3t[1], right)
    parity = (iota((256, 128), 1) & 32) == 0
    out_s[...] = jnp.where(parity, even, odd).astype(BF).reshape(shards, 2 * size, 128)

    third = []
    for k in range(1, shards):
        there = at(0, k)
        third.append(pltpu.make_async_remote_copy(
            src_ref=out_s.at[there["yz"]], dst_ref=in_s.at[s], send_sem=s3.at[k], recv_sem=r3.at[s],
            device_id=there, device_id_type=MESH))
    hear(len(rounds) - 1)
    for copy in third:
        copy.start()
    in_s[s] = out_s[s]
    each(first, sent, 1)
    each(second, sent, 1)

    low = iota((size, 128), 1) < 64
    parity = (iota((size, 128), 1) & 32) == 0
    nothing = jnp.zeros((size, 128), F32)
    main, cross = [], [nothing]
    for n in range(shards + 1):
        if n < shards:
            @pl.when(n != s)
            def _():
                pltpu.make_async_remote_copy(
                    src_ref=out_s.at[0], dst_ref=in_s.at[n], send_sem=s3.at[0], recv_sem=r3.at[n],
                    device_id=at(0, 1), device_id_type=MESH).wait_recv()
            block = in_s[n].astype(F32)
            main.append(block[0:size])
            cross.append(block[size:])
        else:
            cross.append(nothing)
        if n >= 2 and n % 2 == 0:
            left, right = [
                jnp.maximum(main[m] + jnp.where(parity, cross[m], cross[m + 2]), 0.0) for m in (n - 2, n - 1)]
            lanes = slice(n * 64 - 128, n * 64)
            o_ref[0, :, lanes] = jnp.where(low, left, pltpu.roll(right, 64, 1)).astype(BF)
            o_ref[1, :, lanes] = jnp.where(low, pltpu.roll(left, 64, 1), right).astype(BF)
    for copy in third:
        copy.wait_send()


def per_device(volume, weight_one, weight_two, weight_three):
    groups, shards = lax.axis_size("gx"), lax.axis_size("yz")
    size = 128 // shards
    anywhere = pl.BlockSpec(memory_space=pl.ANY)
    dma = pltpu.SemaphoreType.DMA
    out = pl.pallas_call(
        functools.partial(kernel, groups, shards),
        out_shape=jax.ShapeDtypeStruct((2, size, shards * 64), BF),
        in_specs=[anywhere] * 4,
        out_specs=pl.BlockSpec(memory_space=pltpu.VMEM),
        scratch_shapes=[
            pltpu.VMEM((10, 160, 128), BF),
            pltpu.VMEM((32, 432), BF),
            pltpu.VMEM((64, 864), BF),
            pltpu.VMEM((1728, 128), BF),
            pltpu.VMEM((2, 8, 16, 128), BF),
            pltpu.VMEM((10, 480, 128), BF),
            pltpu.VMEM((3, 256, 480), BF),
            pltpu.VMEM((6, 192, 128), BF),
            pltpu.VMEM((4, 576, 128), BF),
            pltpu.VMEM((5, 576, 128), BF),
            pltpu.VMEM((3, 256, 576), BF),
            pltpu.VMEM((2, 256, 1152), BF),
            pltpu.VMEM((shards, 2 * size, 128), BF),
            pltpu.VMEM((shards, 2 * size, 128), BF),
            dma((4,)),
            dma((8,)), dma((8,)), dma((8,)), dma((8,)),
            dma((shards,)), dma((shards,)),
            pltpu.SemaphoreType.REGULAR((8, 2)),
        ],
        compiler_params=pltpu.CompilerParams(collective_id=0, has_side_effects=True),
    )(volume.reshape(8, 128, 128), weight_one, weight_two, weight_three.T)
    return jnp.moveaxis(out, 0, 1)


def solution(mesh):
    placed = (P("gx", None, "yz", None), P(), P(), P())
    return jax.shard_map(
        per_device, mesh=mesh, in_specs=placed, out_specs=P("yz", "gx", None), check_vma=False
    )
```

```python
import functools

import jax
import jax.numpy as jnp
from jax import lax
from jax.experimental import pallas as pl
from jax.experimental.pallas import tpu as pltpu
from jax.sharding import PartitionSpec as P

MESH = pl.DeviceIdType.MESH
BF = jnp.bfloat16
F32 = jnp.float32
BESIDE = ((-1, 0), (1, 0))
AROUND = ((-1, -1), (-1, 1), (1, -1), (1, 1), (0, -1), (0, 1)) + BESIDE


def iota(shape, axis):
    return lax.broadcasted_iota(jnp.int32, shape, axis)


def start(copy):
    copy.start()


def receive(copy):
    copy.wait_recv()


def sent(copy):
    copy.wait_send()


def choose(rows, target):
    return jnp.where(iota((rows, target.shape[1]), 0) == target, 1.0, 0.0).astype(BF)


def dot(a, b):
    return jnp.dot(a, b, preferred_element_type=F32)


def shifted(block, lane, low, high):
    zero = jnp.zeros_like(block)
    up = jnp.where(lane == low, zero, pltpu.roll(block, 1, 1))
    down = jnp.where(lane == high, zero, pltpu.roll(block, 127, 1))
    return up, down


def spread_one(w1, w1t):
    column = iota((1, 480), 1)
    own = column < 384
    edge = column & 31
    c = jnp.where(own, column >> 7, (column - 384) >> 5)
    y = jnp.where(own, column & 7, jnp.where(edge < 16, -1, 8))
    i = jnp.where(own, (column & 127) >> 3, column & 15)
    for out in range(8):
        b = y - out + 1
        target = jnp.where((b >= 0) & (b <= 2), 32 + b * 48 + c * 16 + i, -1)
        chosen = choose(176, target)
        row = (out % 2) * 128 + (out // 2) * 32
        for a, (start, skip) in enumerate(((0, 32), (128, 16), (256, 0))):
            part = dot(w1[:, start:144 * a + 144], chosen[skip:, :])
            w1t[a, row:row + 32, :] = part.astype(BF)


def spread_two(w2, w2t):
    column = iota((1, 576), 1)
    own = column < 384
    edge = column & 63
    c = jnp.where(own, column >> 7, (column - 384) >> 6)
    y = jnp.where(own, (column & 127) >> 5, jnp.where(edge < 32, -1, 4))
    i = column & 31
    for out in range(4):
        b = y - out + 1
        target = jnp.where((b >= 0) & (b <= 2), 64 + b * 96 + c * 32 + i, -1)
        chosen = choose(352, target)
        row = (out % 2) * 128 + (out // 2) * 64
        for a, (start, skip) in enumerate(((0, 64), (256, 32), (512, 0))):
            part = dot(w2[:, start:288 * a + 288], chosen[skip:, :])
            w2t[a, row:row + 64, :] = part.astype(BF)


def spread_three(shards, w3, w3t):
    column = iota((1, 384), 1)
    c = (column >= 128).astype(jnp.int32) + (column >= 256).astype(jnp.int32)
    pos = column - 128 * c
    y = pos >> 6
    i = pos & 63
    size = 128 // shards
    for t, outs in enumerate(((0, 2), (1, -1))):
        parts = [[], [], []]
        for out in outs:
            b = y - out + 1
            target = jnp.where((b >= 0) & (b <= 2), b * 192 + c * 64 + i, -1)
            chosen = choose(576, target)
            for a in range(3):
                parts[a].append(lax.dot_general(
                    w3[a * 576:(a + 1) * 576, :], chosen, (((0,), (0,)), ((), ())),
                    preferred_element_type=F32))
        for a in range(3):
            both = jnp.stack([p.reshape(shards, size, 384) for p in parts[a]], axis=1)
            w3t[t, :, a * 384:(a + 1) * 384] = both.reshape(256, 384).astype(BF)


def kernel(groups, shards, v_hbm, w1_hbm, w2_hbm, w3_hbm, o_ref,
           p, w1, w2, w3, face, b1, h1, a1, w1t, q, b2e, b2o, h2e, h2o, a2, w2t, w3t, out_s, in_s,
           load_sem, s1, r1, s2, r2, s3, r3, known):
    g = lax.axis_index("gx")
    s = lax.axis_index("yz")
    size = 128 // shards

    def at(dx, dy):
        return {"gx": lax.rem(g + dx + groups, groups), "yz": lax.rem(s + dy + shards, shards)}

    def has(dx, dy):
        x = {-1: g > 0, 0: None, 1: g < groups - 1}[dx]
        y = {-1: s > 0, 0: None, 1: s < shards - 1}[dy]
        return y if x is None else (x if y is None else x & y)

    def each(copies, act, sign, among=AROUND):
        for (dx, dy), copy in zip(AROUND, copies):
            if (dx, dy) in among:
                pl.when(has(sign * dx, sign * dy))(functools.partial(act, copy))

    barrier = pltpu.get_barrier_semaphore()
    count = 0
    for dx, dy in AROUND:
        there = has(dx, dy)
        count = count + there.astype(jnp.int32)
        pl.when(there)(functools.partial(
            pl.semaphore_signal, barrier, inc=1, device_id=at(dx, dy), device_id_type=MESH))

    rounds = []
    while 2 << len(rounds) < shards:
        rounds.append(2 << len(rounds))

    def tell(r):
        for side, d in enumerate((-rounds[r], rounds[r])):
            pl.when((s + d >= 0) & (s + d < shards))(functools.partial(
                pl.semaphore_signal, known.at[r, side], inc=1,
                device_id={"gx": g, "yz": lax.rem(s + d + shards, shards)}, device_id_type=MESH))

    def hear(r):
        for side, d in enumerate((rounds[r], -rounds[r])):
            pl.when((s + d >= 0) & (s + d < shards))(functools.partial(
                pl.semaphore_wait, known.at[r, side], 1))

    loads = [
        pltpu.make_async_copy(v_hbm, p.at[1:9, 0:128], load_sem.at[0]),
        pltpu.make_async_copy(w1_hbm, w1, load_sem.at[1]),
        pltpu.make_async_copy(w2_hbm, w2, load_sem.at[2]),
        pltpu.make_async_copy(w3_hbm, w3, load_sem.at[3]),
    ]
    for load in loads:
        load.start()

    loads[0].wait()
    which = iota((32, 128), 0)
    ends = jnp.where(iota((32, 128), 1) == (which & 15) * 8 + (which >> 4) * 7, 1.0, 0.0).astype(BF)
    for x in range(0, 8, 2):
        cells = dot(ends, jnp.concatenate([p[1 + x, 0:128, :], p[2 + x, 0:128, :]], axis=1)).astype(BF)
        for k in range(2):
            face[0, x + k] = cells[0:16, k * 128:(k + 1) * 128]
            face[1, x + k] = cells[16:32, k * 128:(k + 1) * 128]

    @pl.when(g == 0)
    def _():
        p[0] = jnp.zeros((160, 128), BF)
        q[0:2] = jnp.zeros((2, 192, 128), BF)

    @pl.when(g == groups - 1)
    def _():
        p[9] = jnp.zeros((160, 128), BF)
        q[4:6] = jnp.zeros((2, 192, 128), BF)

    @pl.when(s == 0)
    def _():
        p[:, 128:144, :] = jnp.zeros((10, 16, 128), BF)
        q[:, 128:160, :] = jnp.zeros((6, 32, 128), BF)

    @pl.when(s == shards - 1)
    def _():
        p[:, 144:160, :] = jnp.zeros((10, 16, 128), BF)
        q[:, 160:192, :] = jnp.zeros((6, 32, 128), BF)

    pl.semaphore_wait(barrier, count)

    first = []
    for k, (dx, dy) in enumerate(AROUND):
        plane = 7 if dx > 0 else 0
        to = 0 if dx > 0 else 9
        side = 1 if dy > 0 else 0
        rows = slice(128, 144) if dy > 0 else slice(144, 160)
        if dy == 0:
            src, dst = p.at[1 + plane, 0:128], p.at[to, 0:128]
        elif dx == 0:
            src, dst = face.at[side], p.at[1:9, rows]
        else:
            src, dst = face.at[side, plane], p.at[to, rows]
        first.append(pltpu.make_async_remote_copy(
            src_ref=src, dst_ref=dst, send_sem=s1.at[k], recv_sem=r1.at[k],
            device_id=at(dx, dy), device_id_type=MESH))
    each(first, start, 1)

    loads[1].wait()
    spread_one(w1, w1t)
    loads[2].wait()
    spread_two(w2, w2t)

    lane = iota((128, 128), 1)
    narrow = iota((32, 128), 1)

    def lay_one(x):
        mid = p[x, 0:128, :]
        up, down = shifted(mid, lane, 0, 127)
        b1[x, 0:128] = up
        b1[x, 128:256] = mid
        b1[x, 256:384] = down

    def two(ref, x):
        return jnp.concatenate([ref[x], ref[x + 1]], axis=1)

    for x in range(1, 9):
        lay_one(x)
    for k, taps in enumerate(((1, 2), (0, 1, 2), (0, 1, 2), (0, 1))):
        total = None
        for a in taps:
            part = dot(w1t[a, :, 0:384], two(b1, 2 * k + a))
            total = part if total is None else total + part
        a1[k] = total
    a1[0, :, 128:256] += dot(w1t[0, :, 0:384], b1[1])
    a1[3, :, 0:128] += dot(w1t[2, :, 0:384], b1[8])

    each(first, receive, -1, BESIDE)
    lay_one(0)
    lay_one(9)
    a1[0, :, 0:128] += dot(w1t[0, :, 0:384], b1[0])
    a1[3, :, 128:256] += dot(w1t[2, :, 0:384], b1[9])
    each(first, receive, -1, AROUND[:6])
    tell(0)
    for x in range(10):
        mid = p[x, 128:160, :]
        up, down = shifted(mid, narrow, 0, 127)
        h1[x, 0:32] = up
        h1[x, 32:64] = mid
        h1[x, 64:96] = down
    lanes = iota((256, 128), 1)
    pick = jnp.where(iota((256, 128), 0) == (lanes >> 6) * 128 + (lanes & 63) * 2, 1.0, 0.0).astype(BF)

    second = []
    for j in range(2):
        pooled = []
        for k in (2 * j, 2 * j + 1):
            total = a1[k]
            for a in range(3):
                total += dot(w1t[a, :, 384:480], two(h1, 2 * k + a))
            total = jnp.maximum(total, 0.0)
            total = total[0:128] + total[128:256]
            total = total[:, 0:128] + total[:, 128:256]
            total = (total + pltpu.roll(total, 127, 1)) * 0.125
            pooled.append(total.astype(BF))
        q[2 + j, 0:128, :] = dot(jnp.concatenate(pooled, axis=1), pick).astype(BF)
        half = []
        for k, (dx, dy) in enumerate(AROUND):
            to = 2 + j - 2 * dx
            if dy == 0:
                rows, into = slice(0, 128), slice(0, 128)
            elif dy > 0:
                rows, into = slice(96, 128), slice(128, 160)
            else:
                rows, into = slice(0, 32), slice(160, 192)
            half.append(pltpu.make_async_remote_copy(
                src_ref=q.at[2 + j, rows], dst_ref=q.at[to, into], send_sem=s2.at[8 * j + k],
                recv_sem=r2.at[8 * j + k], device_id=at(dx, dy), device_id_type=MESH))
        each(half, start, 1)
        second.append(half)

    loads[3].wait()
    spread_three(shards, w3, w3t)

    for r in range(len(rounds) - 1):
        hear(r)
        tell(r + 1)
    lane = iota((128, 128), 1) & 63
    low = iota((128, 128), 1) < 64

    def lay_two(even, odd, rows, size, lane, low):
        for j in range(5):
            if j > 0:
                mid = q[j, rows, :]
                up, down = shifted(mid, lane, 0, 63)
                even[j - 1, 0:size] = up
                even[j - 1, size:2 * size] = mid
                even[j - 1, 2 * size:3 * size] = down
            mid = jnp.where(low, pltpu.roll(q[j, rows, :], 64, 1), pltpu.roll(q[j + 1, rows, :], 64, 1))
            up, down = shifted(mid, lane, 0, 63)
            odd[j, 0:size] = up
            odd[j, size:2 * size] = mid
            odd[j, 2 * size:3 * size] = down

    def terms_two(even, odd, j, columns):
        total = dot(w2t[0, :, columns], two(odd, j))
        total += dot(w2t[1, :, columns], two(even, j))
        return total + dot(w2t[2, :, columns], two(odd, j + 1))

    for half in second:
        each(half, receive, -1, BESIDE)
    lay_two(b2e, b2o, slice(0, 128), 128, lane, low)
    for j in range(2):
        a2[j] = terms_two(b2e, b2o, 2 * j, slice(0, 384))
    for half in second:
        each(half, receive, -1, AROUND[:6])
    lay_two(h2e, h2o, slice(128, 192), 64, lane[0:64], low[0:64])
    pooled = []
    for j in range(0, 4, 2):
        total = a2[j // 2] + terms_two(h2e, h2o, j, slice(384, 576))
        total = jnp.maximum(total, 0.0)
        total = total[0:128] + total[128:256]
        for k in range(2):
            pair = total[:, k * 128:(k + 1) * 128]
            pair = pair + pltpu.roll(pair, 64, 1)
            pair = (pair + pltpu.roll(pair, 127, 1)) * 0.125
            if j + k == 0:
                pair = jnp.where(g == 0, 0.0, pair)
            if j + k == 3:
                pair = jnp.where(g == groups - 1, 0.0, pair)
            pooled.append(pair)

    stacked = jnp.concatenate(
        [jnp.where(low, pooled[a], pooled[a + 1]).astype(BF) for a in range(3)], axis=0)
    column = iota((1, 384), 1)
    c = column >> 7
    inside = column & 127
    z = (inside & 31) + c - 1
    target = jnp.where((z >= 0) & (z < 32), (inside >> 6) * 64 + 2 * z, -1)
    planes = dot(stacked, choose(128, target)).astype(BF)
    right = jnp.concatenate(
        [planes[a * 128:(a + 1) * 128, c * 128:(c + 1) * 128] for a in range(3) for c in range(3)], axis=0)
    even = dot(w3t[0], right)
    odd = dot(w3t[1], right)
    parity = (iota((256, 128), 1) & 32) == 0
    out_s[...] = jnp.where(parity, even, odd).astype(BF).reshape(shards, 2 * size, 128)

    third = []
    deep = shards // 2
    far = sorted(range(deep), key=lambda d: -min(d, deep - d))
    for flip in (1, 0):
        for d in far:
            if (flip, d) == (0, 0):
                continue
            z = lax.rem(lax.div(s, 2) + d, deep)
            there = 2 * z + (1 - lax.rem(s, 2) if flip else lax.rem(s, 2))
            third.append(pltpu.make_async_remote_copy(
                src_ref=out_s.at[there], dst_ref=in_s.at[s], send_sem=s3.at[len(third)], recv_sem=r3.at[s],
                device_id={"gx": g, "yz": there}, device_id_type=MESH))
    hear(len(rounds) - 1)
    for copy in third:
        copy.start()
    in_s[s] = out_s[s]
    each(first, sent, 1)
    for half in second:
        each(half, sent, 1)

    low = iota((size, 128), 1) < 64
    parity = (iota((size, 128), 1) & 32) == 0
    nothing = jnp.zeros((size, 128), F32)
    main, cross = [], [nothing]
    for n in range(shards + 1):
        if n < shards:
            @pl.when(n != s)
            def _():
                pltpu.make_async_remote_copy(
                    src_ref=out_s.at[0], dst_ref=in_s.at[n], send_sem=s3.at[0], recv_sem=r3.at[n],
                    device_id=at(0, 1), device_id_type=MESH).wait_recv()
            block = in_s[n].astype(F32)
            main.append(block[0:size])
            cross.append(block[size:])
        else:
            cross.append(nothing)
        if n >= 2 and n % 2 == 0:
            left, right = [
                jnp.maximum(main[m] + jnp.where(parity, cross[m], cross[m + 2]), 0.0) for m in (n - 2, n - 1)]
            lanes = slice(n * 64 - 128, n * 64)
            o_ref[0, :, lanes] = jnp.where(low, left, pltpu.roll(right, 64, 1)).astype(BF)
            o_ref[1, :, lanes] = jnp.where(low, pltpu.roll(left, 64, 1), right).astype(BF)
    for copy in third:
        copy.wait_send()


def per_device(volume, weight_one, weight_two, weight_three):
    groups, shards = lax.axis_size("gx"), lax.axis_size("yz")
    size = 128 // shards
    anywhere = pl.BlockSpec(memory_space=pl.ANY)
    dma = pltpu.SemaphoreType.DMA
    out = pl.pallas_call(
        functools.partial(kernel, groups, shards),
        out_shape=jax.ShapeDtypeStruct((2, size, shards * 64), BF),
        in_specs=[anywhere] * 4,
        out_specs=pl.BlockSpec(memory_space=pltpu.VMEM),
        scratch_shapes=[
            pltpu.VMEM((10, 160, 128), BF),
            pltpu.VMEM((32, 432), BF),
            pltpu.VMEM((64, 864), BF),
            pltpu.VMEM((1728, 128), BF),
            pltpu.VMEM((2, 8, 16, 128), BF),
            pltpu.VMEM((10, 384, 128), BF),
            pltpu.VMEM((10, 96, 128), BF),
            pltpu.VMEM((4, 256, 256), F32),
            pltpu.VMEM((3, 256, 480), BF),
            pltpu.VMEM((6, 192, 128), BF),
            pltpu.VMEM((4, 384, 128), BF),
            pltpu.VMEM((5, 384, 128), BF),
            pltpu.VMEM((4, 192, 128), BF),
            pltpu.VMEM((5, 192, 128), BF),
            pltpu.VMEM((2, 256, 256), F32),
            pltpu.VMEM((3, 256, 576), BF),
            pltpu.VMEM((2, 256, 1152), BF),
            pltpu.VMEM((shards, 2 * size, 128), BF),
            pltpu.VMEM((shards, 2 * size, 128), BF),
            dma((4,)),
            dma((8,)), dma((8,)), dma((16,)), dma((16,)),
            dma((shards,)), dma((shards,)),
            pltpu.SemaphoreType.REGULAR((8, 2)),
        ],
        compiler_params=pltpu.CompilerParams(collective_id=0, has_side_effects=True),
    )(volume.reshape(8, 128, 128), weight_one, weight_two, weight_three.T)
    return jnp.moveaxis(out, 0, 1)


def solution(mesh):
    placed = (P("gx", None, "yz", None), P(), P(), P())
    return jax.shard_map(
        per_device, mesh=mesh, in_specs=placed, out_specs=P("yz", "gx", None), check_vma=False
    )
```

```python
import functools

import jax
import jax.numpy as jnp
from jax import lax
from jax.experimental import pallas as pl
from jax.experimental.pallas import tpu as pltpu
from jax.sharding import PartitionSpec as P

MESH = pl.DeviceIdType.MESH
BF = jnp.bfloat16
F32 = jnp.float32
BESIDE = ((-1, 0), (1, 0))
AROUND = ((-1, -1), (-1, 1), (1, -1), (1, 1), (0, -1), (0, 1)) + BESIDE


def iota(shape, axis):
    return lax.broadcasted_iota(jnp.int32, shape, axis)


def start(copy):
    copy.start()


def receive(copy):
    copy.wait_recv()


def sent(copy):
    copy.wait_send()


def choose(rows, target):
    return jnp.where(iota((rows, target.shape[1]), 0) == target, 1.0, 0.0).astype(BF)


def dot(a, b):
    return jnp.dot(a, b, preferred_element_type=F32)


def shifted(block, lane, low, high):
    zero = jnp.zeros_like(block)
    up = jnp.where(lane == low, zero, pltpu.roll(block, 1, 1))
    down = jnp.where(lane == high, zero, pltpu.roll(block, 127, 1))
    return up, down


def spread_one(w1, w1t):
    column = iota((1, 480), 1)
    own = column < 384
    edge = column & 31
    c = jnp.where(own, column >> 7, (column - 384) >> 5)
    y = jnp.where(own, column & 7, jnp.where(edge < 16, -1, 8))
    i = jnp.where(own, (column & 127) >> 3, column & 15)
    for out in range(8):
        b = y - out + 1
        target = jnp.where((b >= 0) & (b <= 2), 32 + b * 48 + c * 16 + i, -1)
        chosen = choose(176, target)
        row = (out % 2) * 128 + (out // 2) * 32
        for a, (start, skip) in enumerate(((0, 32), (128, 16), (256, 0))):
            part = dot(w1[:, start:144 * a + 144], chosen[skip:, :])
            w1t[a, row:row + 32, :] = part.astype(BF)


def spread_two(w2, w2t):
    column = iota((1, 576), 1)
    own = column < 384
    edge = column & 63
    c = jnp.where(own, column >> 7, (column - 384) >> 6)
    y = jnp.where(own, (column & 127) >> 5, jnp.where(edge < 32, -1, 4))
    i = column & 31
    for out in range(4):
        b = y - out + 1
        target = jnp.where((b >= 0) & (b <= 2), 64 + b * 96 + c * 32 + i, -1)
        chosen = choose(352, target)
        row = (out % 2) * 128 + (out // 2) * 64
        for a, (start, skip) in enumerate(((0, 64), (256, 32), (512, 0))):
            part = dot(w2[:, start:288 * a + 288], chosen[skip:, :])
            w2t[a, row:row + 64, :] = part.astype(BF)


def spread_three(shards, w3, w3t):
    column = iota((1, 384), 1)
    c = (column >= 128).astype(jnp.int32) + (column >= 256).astype(jnp.int32)
    pos = column - 128 * c
    y = pos >> 6
    i = pos & 63
    size = 128 // shards
    for t, outs in enumerate(((0, 2), (1, -1))):
        parts = [[], [], []]
        for out in outs:
            b = y - out + 1
            target = jnp.where((b >= 0) & (b <= 2), b * 192 + c * 64 + i, -1)
            chosen = choose(576, target)
            for a in range(3):
                parts[a].append(lax.dot_general(
                    w3[a * 576:(a + 1) * 576, :], chosen, (((0,), (0,)), ((), ())),
                    preferred_element_type=F32))
        for a in range(3):
            both = jnp.stack([p.reshape(shards, size, 384) for p in parts[a]], axis=1)
            w3t[t, :, a * 384:(a + 1) * 384] = both.reshape(256, 384).astype(BF)


def kernel(groups, shards, v_hbm, w1_hbm, w2_hbm, w3_hbm, o_ref,
           p, w1, w2, w3, face, b1, h1, a1, w1t, q, b2e, b2o, h2e, h2o, a2, w2t, w3t, out_s, in_s,
           load_sem, s1, r1, s2, r2, s3, r3, known):
    g = lax.axis_index("gx")
    s = lax.axis_index("yz")
    size = 128 // shards

    def at(dx, dy):
        return {"gx": lax.rem(g + dx + groups, groups), "yz": lax.rem(s + dy + shards, shards)}

    def has(dx, dy):
        x = {-1: g > 0, 0: None, 1: g < groups - 1}[dx]
        y = {-1: s > 0, 0: None, 1: s < shards - 1}[dy]
        return y if x is None else (x if y is None else x & y)

    def each(copies, act, sign, among=AROUND):
        for (dx, dy), copy in zip(AROUND, copies):
            if (dx, dy) in among:
                pl.when(has(sign * dx, sign * dy))(functools.partial(act, copy))

    barrier = pltpu.get_barrier_semaphore()
    count = 0
    for dx, dy in AROUND:
        there = has(dx, dy)
        count = count + there.astype(jnp.int32)
        pl.when(there)(functools.partial(
            pl.semaphore_signal, barrier, inc=1, device_id=at(dx, dy), device_id_type=MESH))

    rounds = []
    while 2 << len(rounds) < shards:
        rounds.append(2 << len(rounds))

    def tell(r):
        for side, d in enumerate((-rounds[r], rounds[r])):
            pl.when((s + d >= 0) & (s + d < shards))(functools.partial(
                pl.semaphore_signal, known.at[r, side], inc=1,
                device_id={"gx": g, "yz": lax.rem(s + d + shards, shards)}, device_id_type=MESH))

    def hear(r):
        for side, d in enumerate((rounds[r], -rounds[r])):
            pl.when((s + d >= 0) & (s + d < shards))(functools.partial(
                pl.semaphore_wait, known.at[r, side], 1))

    loads = [
        pltpu.make_async_copy(v_hbm, p.at[1:9, 0:128], load_sem.at[0]),
        pltpu.make_async_copy(w1_hbm, w1, load_sem.at[1]),
        pltpu.make_async_copy(w2_hbm, w2, load_sem.at[2]),
        pltpu.make_async_copy(w3_hbm, w3, load_sem.at[3]),
    ]
    for load in loads:
        load.start()

    loads[0].wait()
    which = iota((32, 128), 0)
    ends = jnp.where(iota((32, 128), 1) == (which & 15) * 8 + (which >> 4) * 7, 1.0, 0.0).astype(BF)
    for x in range(0, 8, 2):
        cells = dot(ends, jnp.concatenate([p[1 + x, 0:128, :], p[2 + x, 0:128, :]], axis=1)).astype(BF)
        for k in range(2):
            face[0, x + k] = cells[0:16, k * 128:(k + 1) * 128]
            face[1, x + k] = cells[16:32, k * 128:(k + 1) * 128]

    @pl.when(g == 0)
    def _():
        p[0] = jnp.zeros((160, 128), BF)
        q[0:2] = jnp.zeros((2, 192, 128), BF)

    @pl.when(g == groups - 1)
    def _():
        p[9] = jnp.zeros((160, 128), BF)
        q[4:6] = jnp.zeros((2, 192, 128), BF)

    @pl.when(s == 0)
    def _():
        p[:, 128:144, :] = jnp.zeros((10, 16, 128), BF)
        q[:, 128:160, :] = jnp.zeros((6, 32, 128), BF)

    @pl.when(s == shards - 1)
    def _():
        p[:, 144:160, :] = jnp.zeros((10, 16, 128), BF)
        q[:, 160:192, :] = jnp.zeros((6, 32, 128), BF)

    pl.semaphore_wait(barrier, count)

    first = []
    for k, (dx, dy) in enumerate(AROUND):
        plane = 7 if dx > 0 else 0
        to = 0 if dx > 0 else 9
        side = 1 if dy > 0 else 0
        rows = slice(128, 144) if dy > 0 else slice(144, 160)
        if dy == 0:
            src, dst = p.at[1 + plane, 0:128], p.at[to, 0:128]
        elif dx == 0:
            src, dst = face.at[side], p.at[1:9, rows]
        else:
            src, dst = face.at[side, plane], p.at[to, rows]
        first.append(pltpu.make_async_remote_copy(
            src_ref=src, dst_ref=dst, send_sem=s1.at[k], recv_sem=r1.at[k],
            device_id=at(dx, dy), device_id_type=MESH))
    each(first, start, 1)

    loads[1].wait()
    spread_one(w1, w1t)
    loads[2].wait()
    spread_two(w2, w2t)

    lane = iota((128, 128), 1)
    narrow = iota((32, 128), 1)

    def lay_one(x):
        mid = p[x, 0:128, :]
        up, down = shifted(mid, lane, 0, 127)
        b1[x, 0:128] = up
        b1[x, 128:256] = mid
        b1[x, 256:384] = down

    def two(ref, x):
        return jnp.concatenate([ref[x], ref[x + 1]], axis=1)

    for x in range(1, 9):
        lay_one(x)
    for k, taps in enumerate(((1, 2), (0, 1, 2), (0, 1, 2), (0, 1))):
        total = None
        for a in taps:
            part = dot(w1t[a, :, 0:384], two(b1, 2 * k + a))
            total = part if total is None else total + part
        a1[k] = total
    a1[0, :, 128:256] += dot(w1t[0, :, 0:384], b1[1])
    a1[3, :, 0:128] += dot(w1t[2, :, 0:384], b1[8])

    lanes = iota((256, 128), 1)
    pick = jnp.where(iota((256, 128), 0) == (lanes >> 6) * 128 + (lanes & 63) * 2, 1.0, 0.0).astype(BF)

    each(first, receive, -1, BESIDE)
    lay_one(0)
    lay_one(9)
    a1[0, :, 0:128] += dot(w1t[0, :, 0:384], b1[0])
    a1[3, :, 128:256] += dot(w1t[2, :, 0:384], b1[9])

    def edge_one(x):
        mid = p[x, 128:160, :]
        up, down = shifted(mid, narrow, 0, 127)
        h1[x, 0:32] = up
        h1[x, 32:64] = mid
        h1[x, 64:96] = down

    def edge_terms(k, taps):
        total = a1[k]
        for a in taps:
            total += dot(w1t[a, :, 384:480], two(h1, 2 * k + a))
        return total

    def pool_one(total):
        total = jnp.maximum(total, 0.0)
        total = total[0:128] + total[128:256]
        total = total[:, 0:128] + total[:, 128:256]
        return ((total + pltpu.roll(total, 127, 1)) * 0.125).astype(BF)

    each(first, receive, -1, AROUND[4:6])
    for x in range(1, 9):
        edge_one(x)
    inner = [pool_one(edge_terms(k, (0, 1, 2))) for k in (1, 2)]
    a1[0] = edge_terms(0, (1, 2))
    a1[3] = edge_terms(3, (0, 1))
    each(first, receive, -1, AROUND[:4])

    second = []
    for j in range(2):
        edge_one(9 * j)
        outer = pool_one(edge_terms(3 * j, (2 * j,)))
        pooled = [inner[1], outer] if j else [outer, inner[0]]
        q[2 + j, 0:128, :] = dot(jnp.concatenate(pooled, axis=1), pick).astype(BF)
        half = []
        for k, (dx, dy) in enumerate(AROUND):
            to = 2 + j - 2 * dx
            if dy == 0:
                rows, into = slice(0, 128), slice(0, 128)
            elif dy > 0:
                rows, into = slice(96, 128), slice(128, 160)
            else:
                rows, into = slice(0, 32), slice(160, 192)
            half.append(pltpu.make_async_remote_copy(
                src_ref=q.at[2 + j, rows], dst_ref=q.at[to, into], send_sem=s2.at[8 * j + k],
                recv_sem=r2.at[8 * j + k], device_id=at(dx, dy), device_id_type=MESH))
        each(half, start, 1)
        second.append(half)

    tell(0)
    loads[3].wait()
    spread_three(shards, w3, w3t)

    for r in range(len(rounds) - 1):
        hear(r)
        tell(r + 1)
    lane = iota((128, 128), 1) & 63
    low = iota((128, 128), 1) < 64

    def lay_two(even, odd, rows, size, lane, low):
        for j in range(5):
            if j > 0:
                mid = q[j, rows, :]
                up, down = shifted(mid, lane, 0, 63)
                even[j - 1, 0:size] = up
                even[j - 1, size:2 * size] = mid
                even[j - 1, 2 * size:3 * size] = down
            mid = jnp.where(low, pltpu.roll(q[j, rows, :], 64, 1), pltpu.roll(q[j + 1, rows, :], 64, 1))
            up, down = shifted(mid, lane, 0, 63)
            odd[j, 0:size] = up
            odd[j, size:2 * size] = mid
            odd[j, 2 * size:3 * size] = down

    def terms_two(even, odd, j, columns):
        total = dot(w2t[0, :, columns], two(odd, j))
        total += dot(w2t[1, :, columns], two(even, j))
        return total + dot(w2t[2, :, columns], two(odd, j + 1))

    column = iota((1, 384), 1)
    c = column >> 7
    inside = column & 127
    z = (inside & 31) + c - 1
    target = jnp.where((z >= 0) & (z < 32), (inside >> 6) * 64 + 2 * z, -1)
    chosen = choose(128, target)

    for half in second:
        each(half, receive, -1, BESIDE)
    lay_two(b2e, b2o, slice(0, 128), 128, lane, low)
    for j in range(2):
        a2[j] = terms_two(b2e, b2o, 2 * j, slice(0, 384))
    for half in second:
        each(half, receive, -1, AROUND[:6])
    lay_two(h2e, h2o, slice(128, 192), 64, lane[0:64], low[0:64])
    pooled = []
    for j in range(0, 4, 2):
        total = a2[j // 2] + terms_two(h2e, h2o, j, slice(384, 576))
        total = jnp.maximum(total, 0.0)
        total = total[0:128] + total[128:256]
        for k in range(2):
            pair = total[:, k * 128:(k + 1) * 128]
            pair = pair + pltpu.roll(pair, 64, 1)
            pair = (pair + pltpu.roll(pair, 127, 1)) * 0.125
            if j + k == 0:
                pair = jnp.where(g == 0, 0.0, pair)
            if j + k == 3:
                pair = jnp.where(g == groups - 1, 0.0, pair)
            pooled.append(pair)

    stacked = jnp.concatenate(
        [jnp.where(low, pooled[a], pooled[a + 1]).astype(BF) for a in range(3)], axis=0)
    planes = dot(stacked, chosen).astype(BF)
    right = jnp.concatenate(
        [planes[a * 128:(a + 1) * 128, c * 128:(c + 1) * 128] for a in range(3) for c in range(3)], axis=0)
    even = dot(w3t[0], right)
    odd = dot(w3t[1], right)
    parity = (iota((256, 128), 1) & 32) == 0
    out_s[...] = jnp.where(parity, even, odd).astype(BF).reshape(shards, 2 * size, 128)

    third = []
    deep = shards // 2
    far = sorted(range(deep), key=lambda d: -min(d, deep - d))
    for flip in (1, 0):
        for d in far:
            if (flip, d) == (0, 0):
                continue
            z = lax.rem(lax.div(s, 2) + d, deep)
            there = 2 * z + (1 - lax.rem(s, 2) if flip else lax.rem(s, 2))
            third.append(pltpu.make_async_remote_copy(
                src_ref=out_s.at[there], dst_ref=in_s.at[s], send_sem=s3.at[len(third)], recv_sem=r3.at[s],
                device_id={"gx": g, "yz": there}, device_id_type=MESH))
    hear(len(rounds) - 1)
    for copy in third:
        copy.start()
    in_s[s] = out_s[s]
    each(first, sent, 1)
    for half in second:
        each(half, sent, 1)

    low = iota((size, 128), 1) < 64
    parity = (iota((size, 128), 1) & 32) == 0
    nothing = jnp.zeros((size, 128), F32)
    main, cross = [], [nothing]
    for n in range(shards + 1):
        if n < shards:
            @pl.when(n != s)
            def _():
                pltpu.make_async_remote_copy(
                    src_ref=out_s.at[0], dst_ref=in_s.at[n], send_sem=s3.at[0], recv_sem=r3.at[n],
                    device_id=at(0, 1), device_id_type=MESH).wait_recv()
            block = in_s[n].astype(F32)
            main.append(block[0:size])
            cross.append(block[size:])
        else:
            cross.append(nothing)
        if n >= 2 and n % 2 == 0:
            left, right = [
                jnp.maximum(main[m] + jnp.where(parity, cross[m], cross[m + 2]), 0.0) for m in (n - 2, n - 1)]
            lanes = slice(n * 64 - 128, n * 64)
            o_ref[0, :, lanes] = jnp.where(low, left, pltpu.roll(right, 64, 1)).astype(BF)
            o_ref[1, :, lanes] = jnp.where(low, pltpu.roll(left, 64, 1), right).astype(BF)
    for copy in third:
        copy.wait_send()


def per_device(volume, weight_one, weight_two, weight_three):
    groups, shards = lax.axis_size("gx"), lax.axis_size("yz")
    size = 128 // shards
    anywhere = pl.BlockSpec(memory_space=pl.ANY)
    dma = pltpu.SemaphoreType.DMA
    out = pl.pallas_call(
        functools.partial(kernel, groups, shards),
        out_shape=jax.ShapeDtypeStruct((2, size, shards * 64), BF),
        in_specs=[anywhere] * 4,
        out_specs=pl.BlockSpec(memory_space=pltpu.VMEM),
        scratch_shapes=[
            pltpu.VMEM((10, 160, 128), BF),
            pltpu.VMEM((32, 432), BF),
            pltpu.VMEM((64, 864), BF),
            pltpu.VMEM((1728, 128), BF),
            pltpu.VMEM((2, 8, 16, 128), BF),
            pltpu.VMEM((10, 384, 128), BF),
            pltpu.VMEM((10, 96, 128), BF),
            pltpu.VMEM((4, 256, 256), F32),
            pltpu.VMEM((3, 256, 480), BF),
            pltpu.VMEM((6, 192, 128), BF),
            pltpu.VMEM((4, 384, 128), BF),
            pltpu.VMEM((5, 384, 128), BF),
            pltpu.VMEM((4, 192, 128), BF),
            pltpu.VMEM((5, 192, 128), BF),
            pltpu.VMEM((2, 256, 256), F32),
            pltpu.VMEM((3, 256, 576), BF),
            pltpu.VMEM((2, 256, 1152), BF),
            pltpu.VMEM((shards, 2 * size, 128), BF),
            pltpu.VMEM((shards, 2 * size, 128), BF),
            dma((4,)),
            dma((8,)), dma((8,)), dma((16,)), dma((16,)),
            dma((shards,)), dma((shards,)),
            pltpu.SemaphoreType.REGULAR((8, 2)),
        ],
        compiler_params=pltpu.CompilerParams(collective_id=0, has_side_effects=True),
    )(volume.reshape(8, 128, 128), weight_one, weight_two, weight_three.T)
    return jnp.moveaxis(out, 0, 1)


def solution(mesh):
    placed = (P("gx", None, "yz", None), P(), P(), P())
    return jax.shard_map(
        per_device, mesh=mesh, in_specs=placed, out_specs=P("yz", "gx", None), check_vma=False
    )
```

```python
import functools

import jax
import jax.numpy as jnp
from jax import lax
from jax.experimental import pallas as pl
from jax.experimental.pallas import tpu as pltpu
from jax.sharding import PartitionSpec as P

MESH = pl.DeviceIdType.MESH
BF = jnp.bfloat16
F32 = jnp.float32
BESIDE = ((-1, 0), (1, 0))
PIECES = ((1, -1, None), (1, 1, None), (0, -1, (0, 5)), (0, 1, (0, 5)), (-1, -1, None), (-1, 1, None),
          (0, -1, (5, 8)), (0, 1, (5, 8)), (-1, 0, None), (1, 0, None))
AROUND = ((-1, -1), (-1, 1), (1, -1), (1, 1), (0, -1), (0, 1)) + BESIDE


def iota(shape, axis):
    return lax.broadcasted_iota(jnp.int32, shape, axis)


def start(copy):
    copy.start()


def receive(copy):
    copy.wait_recv()


def sent(copy):
    copy.wait_send()


def choose(rows, target):
    return jnp.where(iota((rows, target.shape[1]), 0) == target, 1.0, 0.0).astype(BF)


def dot(a, b):
    return jnp.dot(a, b, preferred_element_type=F32)


def shifted(block, lane, low, high):
    zero = jnp.zeros_like(block)
    up = jnp.where(lane == low, zero, pltpu.roll(block, 1, 1))
    down = jnp.where(lane == high, zero, pltpu.roll(block, 127, 1))
    return up, down


def spread_one(w1, w1t):
    column = iota((1, 480), 1)
    own = column < 384
    edge = column & 31
    c = jnp.where(own, column >> 7, (column - 384) >> 5)
    y = jnp.where(own, column & 7, jnp.where(edge < 16, -1, 8))
    i = jnp.where(own, (column & 127) >> 3, column & 15)
    for out in range(8):
        b = y - out + 1
        target = jnp.where((b >= 0) & (b <= 2), 32 + b * 48 + c * 16 + i, -1)
        chosen = choose(176, target)
        row = (out % 2) * 128 + (out // 2) * 32
        for a, (start, skip) in enumerate(((0, 32), (128, 16), (256, 0))):
            part = dot(w1[:, start:144 * a + 144], chosen[skip:, :])
            w1t[a, row:row + 32, :] = part.astype(BF)


def spread_two(w2, w2t):
    column = iota((1, 576), 1)
    own = column < 384
    edge = column & 63
    c = jnp.where(own, column >> 7, (column - 384) >> 6)
    y = jnp.where(own, (column & 127) >> 5, jnp.where(edge < 32, -1, 4))
    i = column & 31
    for out in range(4):
        b = y - out + 1
        target = jnp.where((b >= 0) & (b <= 2), 64 + b * 96 + c * 32 + i, -1)
        chosen = choose(352, target)
        row = (out % 2) * 128 + (out // 2) * 64
        for a, (start, skip) in enumerate(((0, 64), (256, 32), (512, 0))):
            part = dot(w2[:, start:288 * a + 288], chosen[skip:, :])
            w2t[a, row:row + 64, :] = part.astype(BF)


def spread_three(shards, w3, w3t):
    column = iota((1, 384), 1)
    c = (column >= 128).astype(jnp.int32) + (column >= 256).astype(jnp.int32)
    pos = column - 128 * c
    y = pos >> 6
    i = pos & 63
    size = 128 // shards
    for t, outs in enumerate(((0, 2), (1, -1))):
        parts = [[], [], []]
        for out in outs:
            b = y - out + 1
            target = jnp.where((b >= 0) & (b <= 2), b * 192 + c * 64 + i, -1)
            chosen = choose(576, target)
            for a in range(3):
                parts[a].append(lax.dot_general(
                    w3[a * 576:(a + 1) * 576, :], chosen, (((0,), (0,)), ((), ())),
                    preferred_element_type=F32))
        for a in range(3):
            both = jnp.stack([p.reshape(shards, size, 384) for p in parts[a]], axis=1)
            w3t[t, :, a * 384:(a + 1) * 384] = both.reshape(256, 384).astype(BF)


def kernel(groups, shards, v_hbm, w1_hbm, w2_hbm, w3_hbm, o_ref,
           p, w1, w2, w3, face, b1, h1, a1, w1t, q, b2e, b2o, h2e, h2o, a2, w2t, w3t, out_s, in_s,
           load_sem, s1, r1, s2, r2, s3, r3, known):
    g = lax.axis_index("gx")
    s = lax.axis_index("yz")
    size = 128 // shards

    def at(dx, dy):
        return {"gx": lax.rem(g + dx + groups, groups), "yz": lax.rem(s + dy + shards, shards)}

    def has(dx, dy):
        x = {-1: g > 0, 0: None, 1: g < groups - 1}[dx]
        y = {-1: s > 0, 0: None, 1: s < shards - 1}[dy]
        return y if x is None else (x if y is None else x & y)

    def each(copies, act, sign, among=AROUND):
        for (dx, dy), copy in zip(AROUND, copies):
            if (dx, dy) in among:
                pl.when(has(sign * dx, sign * dy))(functools.partial(act, copy))

    def pieces(copies, act, sign, low, high):
        for (dx, dy, _), copy in zip(PIECES[low:high], copies[low:high]):
            pl.when(has(sign * dx, sign * dy))(functools.partial(act, copy))

    barrier = pltpu.get_barrier_semaphore()
    count = 0
    for dx, dy in AROUND:
        there = has(dx, dy)
        count = count + there.astype(jnp.int32)
        pl.when(there)(functools.partial(
            pl.semaphore_signal, barrier, inc=1, device_id=at(dx, dy), device_id_type=MESH))

    rounds = []
    while 2 << len(rounds) < shards:
        rounds.append(2 << len(rounds))

    def tell(r):
        for side, d in enumerate((-rounds[r], rounds[r])):
            pl.when((s + d >= 0) & (s + d < shards))(functools.partial(
                pl.semaphore_signal, known.at[r, side], inc=1,
                device_id={"gx": g, "yz": lax.rem(s + d + shards, shards)}, device_id_type=MESH))

    def hear(r):
        for side, d in enumerate((rounds[r], -rounds[r])):
            pl.when((s + d >= 0) & (s + d < shards))(functools.partial(
                pl.semaphore_wait, known.at[r, side], 1))

    loads = [
        pltpu.make_async_copy(v_hbm, p.at[1:9, 0:128], load_sem.at[0]),
        pltpu.make_async_copy(w1_hbm, w1, load_sem.at[1]),
        pltpu.make_async_copy(w2_hbm, w2, load_sem.at[2]),
        pltpu.make_async_copy(w3_hbm, w3, load_sem.at[3]),
    ]
    for load in loads:
        load.start()

    loads[0].wait()
    which = iota((32, 128), 0)
    ends = jnp.where(iota((32, 128), 1) == (which & 15) * 8 + (which >> 4) * 7, 1.0, 0.0).astype(BF)
    for x in range(0, 8, 2):
        cells = dot(ends, jnp.concatenate([p[1 + x, 0:128, :], p[2 + x, 0:128, :]], axis=1)).astype(BF)
        for k in range(2):
            face[0, x + k] = cells[0:16, k * 128:(k + 1) * 128]
            face[1, x + k] = cells[16:32, k * 128:(k + 1) * 128]

    @pl.when(g == 0)
    def _():
        p[0] = jnp.zeros((160, 128), BF)
        q[0:2] = jnp.zeros((2, 192, 128), BF)

    @pl.when(g == groups - 1)
    def _():
        p[9] = jnp.zeros((160, 128), BF)
        q[4:6] = jnp.zeros((2, 192, 128), BF)

    @pl.when(s == 0)
    def _():
        p[:, 128:144, :] = jnp.zeros((10, 16, 128), BF)
        q[:, 128:160, :] = jnp.zeros((6, 32, 128), BF)

    @pl.when(s == shards - 1)
    def _():
        p[:, 144:160, :] = jnp.zeros((10, 16, 128), BF)
        q[:, 160:192, :] = jnp.zeros((6, 32, 128), BF)

    pl.semaphore_wait(barrier, count)

    first = []
    for k, (dx, dy, part) in enumerate(PIECES):
        plane = 7 if dx > 0 else 0
        to = 0 if dx > 0 else 9
        side = 1 if dy > 0 else 0
        rows = slice(128, 144) if dy > 0 else slice(144, 160)
        if dy == 0:
            src, dst = p.at[1 + plane, 0:128], p.at[to, 0:128]
        elif dx == 0:
            low, high = part
            src, dst = face.at[side, low:high], p.at[1 + low:1 + high, rows]
        else:
            src, dst = face.at[side, plane], p.at[to, rows]
        first.append(pltpu.make_async_remote_copy(
            src_ref=src, dst_ref=dst, send_sem=s1.at[k], recv_sem=r1.at[k],
            device_id=at(dx, dy), device_id_type=MESH))
    pieces(first, start, 1, 0, 10)

    loads[1].wait()
    spread_one(w1, w1t)
    loads[2].wait()
    spread_two(w2, w2t)

    lane = iota((128, 128), 1)
    narrow = iota((32, 128), 1)

    def lay_one(x):
        mid = p[x, 0:128, :]
        up, down = shifted(mid, lane, 0, 127)
        b1[x, 0:128] = up
        b1[x, 128:256] = mid
        b1[x, 256:384] = down

    def two(ref, x):
        return jnp.concatenate([ref[x], ref[x + 1]], axis=1)

    for x in range(1, 9):
        lay_one(x)
    for k, taps in enumerate(((1, 2), (0, 1, 2), (0, 1, 2), (0, 1))):
        total = None
        for a in taps:
            part = dot(w1t[a, :, 0:384], two(b1, 2 * k + a))
            total = part if total is None else total + part
        a1[k] = total
    a1[0, :, 128:256] += dot(w1t[0, :, 0:384], b1[1])
    a1[3, :, 0:128] += dot(w1t[2, :, 0:384], b1[8])

    lanes = iota((256, 128), 1)
    pick = jnp.where(iota((256, 128), 0) == (lanes >> 6) * 128 + (lanes & 63) * 2, 1.0, 0.0).astype(BF)

    pieces(first, receive, -1, 8, 10)
    lay_one(0)
    lay_one(9)
    a1[0, :, 0:128] += dot(w1t[0, :, 0:384], b1[0])
    a1[3, :, 128:256] += dot(w1t[2, :, 0:384], b1[9])
    second = []
    for j in range(2):
        pieces(first, receive, -1, 4 * j, 4 * j + 4)
        for x in range(6 * j, 6 + 4 * j):
            mid = p[x, 128:160, :]
            up, down = shifted(mid, narrow, 0, 127)
            h1[x, 0:32] = up
            h1[x, 32:64] = mid
            h1[x, 64:96] = down
        pooled = []
        for k in (2 * j, 2 * j + 1):
            total = a1[k]
            for a in range(3):
                total += dot(w1t[a, :, 384:480], two(h1, 2 * k + a))
            total = jnp.maximum(total, 0.0)
            total = total[0:128] + total[128:256]
            total = total[:, 0:128] + total[:, 128:256]
            total = (total + pltpu.roll(total, 127, 1)) * 0.125
            pooled.append(total.astype(BF))
        q[2 + j, 0:128, :] = dot(jnp.concatenate(pooled, axis=1), pick).astype(BF)
        half = []
        for k, (dx, dy) in enumerate(AROUND):
            to = 2 + j - 2 * dx
            if dy == 0:
                rows, into = slice(0, 128), slice(0, 128)
            elif dy > 0:
                rows, into = slice(96, 128), slice(128, 160)
            else:
                rows, into = slice(0, 32), slice(160, 192)
            half.append(pltpu.make_async_remote_copy(
                src_ref=q.at[2 + j, rows], dst_ref=q.at[to, into], send_sem=s2.at[8 * j + k],
                recv_sem=r2.at[8 * j + k], device_id=at(dx, dy), device_id_type=MESH))
        each(half, start, 1)
        second.append(half)

    tell(0)
    loads[3].wait()
    spread_three(shards, w3, w3t)

    for r in range(len(rounds) - 1):
        hear(r)
        tell(r + 1)
    lane = iota((128, 128), 1) & 63
    low = iota((128, 128), 1) < 64

    def lay_two(even, odd, rows, size, lane, low):
        for j in range(5):
            if j > 0:
                mid = q[j, rows, :]
                up, down = shifted(mid, lane, 0, 63)
                even[j - 1, 0:size] = up
                even[j - 1, size:2 * size] = mid
                even[j - 1, 2 * size:3 * size] = down
            mid = jnp.where(low, pltpu.roll(q[j, rows, :], 64, 1), pltpu.roll(q[j + 1, rows, :], 64, 1))
            up, down = shifted(mid, lane, 0, 63)
            odd[j, 0:size] = up
            odd[j, size:2 * size] = mid
            odd[j, 2 * size:3 * size] = down

    def terms_two(even, odd, j, columns):
        total = dot(w2t[0, :, columns], two(odd, j))
        total += dot(w2t[1, :, columns], two(even, j))
        return total + dot(w2t[2, :, columns], two(odd, j + 1))

    column = iota((1, 384), 1)
    c = column >> 7
    inside = column & 127
    z = (inside & 31) + c - 1
    target = jnp.where((z >= 0) & (z < 32), (inside >> 6) * 64 + 2 * z, -1)
    chosen = choose(128, target)

    for half in second:
        each(half, receive, -1, BESIDE)
    lay_two(b2e, b2o, slice(0, 128), 128, lane, low)
    for j in range(2):
        a2[j] = terms_two(b2e, b2o, 2 * j, slice(0, 384))
    for half in second:
        each(half, receive, -1, AROUND[:6])
    lay_two(h2e, h2o, slice(128, 192), 64, lane[0:64], low[0:64])
    pooled = []
    for j in range(0, 4, 2):
        total = a2[j // 2] + terms_two(h2e, h2o, j, slice(384, 576))
        total = jnp.maximum(total, 0.0)
        total = total[0:128] + total[128:256]
        for k in range(2):
            pair = total[:, k * 128:(k + 1) * 128]
            pair = pair + pltpu.roll(pair, 64, 1)
            pair = (pair + pltpu.roll(pair, 127, 1)) * 0.125
            if j + k == 0:
                pair = jnp.where(g == 0, 0.0, pair)
            if j + k == 3:
                pair = jnp.where(g == groups - 1, 0.0, pair)
            pooled.append(pair)

    stacked = jnp.concatenate(
        [jnp.where(low, pooled[a], pooled[a + 1]).astype(BF) for a in range(3)], axis=0)
    planes = dot(stacked, chosen).astype(BF)
    right = jnp.concatenate(
        [planes[a * 128:(a + 1) * 128, c * 128:(c + 1) * 128] for a in range(3) for c in range(3)], axis=0)
    even = dot(w3t[0], right)
    odd = dot(w3t[1], right)
    parity = (iota((256, 128), 1) & 32) == 0
    out_s[...] = jnp.where(parity, even, odd).astype(BF).reshape(shards, 2 * size, 128)

    third = []
    deep = shards // 2
    far = sorted(range(deep), key=lambda d: -min(d, deep - d))
    for flip in (1, 0):
        for d in far:
            if (flip, d) == (0, 0):
                continue
            z = lax.rem(lax.div(s, 2) + d, deep)
            there = 2 * z + (1 - lax.rem(s, 2) if flip else lax.rem(s, 2))
            third.append(pltpu.make_async_remote_copy(
                src_ref=out_s.at[there], dst_ref=in_s.at[s], send_sem=s3.at[len(third)], recv_sem=r3.at[s],
                device_id={"gx": g, "yz": there}, device_id_type=MESH))
    hear(len(rounds) - 1)
    for copy in third:
        copy.start()
    in_s[s] = out_s[s]
    pieces(first, sent, 1, 0, 10)
    for half in second:
        each(half, sent, 1)

    low = iota((size, 128), 1) < 64
    parity = (iota((size, 128), 1) & 32) == 0
    nothing = jnp.zeros((size, 128), F32)
    main, cross = [], [nothing]
    for n in range(shards + 1):
        if n < shards:
            @pl.when(n != s)
            def _():
                pltpu.make_async_remote_copy(
                    src_ref=out_s.at[0], dst_ref=in_s.at[n], send_sem=s3.at[0], recv_sem=r3.at[n],
                    device_id=at(0, 1), device_id_type=MESH).wait_recv()
            block = in_s[n].astype(F32)
            main.append(block[0:size])
            cross.append(block[size:])
        else:
            cross.append(nothing)
        if n >= 2 and n % 2 == 0:
            left, right = [
                jnp.maximum(main[m] + jnp.where(parity, cross[m], cross[m + 2]), 0.0) for m in (n - 2, n - 1)]
            lanes = slice(n * 64 - 128, n * 64)
            o_ref[0, :, lanes] = jnp.where(low, left, pltpu.roll(right, 64, 1)).astype(BF)
            o_ref[1, :, lanes] = jnp.where(low, pltpu.roll(left, 64, 1), right).astype(BF)
    for copy in third:
        copy.wait_send()


def per_device(volume, weight_one, weight_two, weight_three):
    groups, shards = lax.axis_size("gx"), lax.axis_size("yz")
    size = 128 // shards
    anywhere = pl.BlockSpec(memory_space=pl.ANY)
    dma = pltpu.SemaphoreType.DMA
    out = pl.pallas_call(
        functools.partial(kernel, groups, shards),
        out_shape=jax.ShapeDtypeStruct((2, size, shards * 64), BF),
        in_specs=[anywhere] * 4,
        out_specs=pl.BlockSpec(memory_space=pltpu.VMEM),
        scratch_shapes=[
            pltpu.VMEM((10, 160, 128), BF),
            pltpu.VMEM((32, 432), BF),
            pltpu.VMEM((64, 864), BF),
            pltpu.VMEM((1728, 128), BF),
            pltpu.VMEM((2, 8, 16, 128), BF),
            pltpu.VMEM((10, 384, 128), BF),
            pltpu.VMEM((10, 96, 128), BF),
            pltpu.VMEM((4, 256, 256), F32),
            pltpu.VMEM((3, 256, 480), BF),
            pltpu.VMEM((6, 192, 128), BF),
            pltpu.VMEM((4, 384, 128), BF),
            pltpu.VMEM((5, 384, 128), BF),
            pltpu.VMEM((4, 192, 128), BF),
            pltpu.VMEM((5, 192, 128), BF),
            pltpu.VMEM((2, 256, 256), F32),
            pltpu.VMEM((3, 256, 576), BF),
            pltpu.VMEM((2, 256, 1152), BF),
            pltpu.VMEM((shards, 2 * size, 128), BF),
            pltpu.VMEM((shards, 2 * size, 128), BF),
            dma((4,)),
            dma((10,)), dma((10,)), dma((16,)), dma((16,)),
            dma((shards,)), dma((shards,)),
            pltpu.SemaphoreType.REGULAR((8, 2)),
        ],
        compiler_params=pltpu.CompilerParams(
            collective_id=0, has_side_effects=True, vmem_limit_bytes=56510000),
    )(volume.reshape(8, 128, 128), weight_one, weight_two, weight_three.T)
    return jnp.moveaxis(out, 0, 1)


def solution(mesh):
    placed = (P("gx", None, "yz", None), P(), P(), P())
    return jax.shard_map(
        per_device, mesh=mesh, in_specs=placed, out_specs=P("yz", "gx", None), check_vma=False
    )
```

```python
import functools

import jax
import jax.numpy as jnp
from jax import lax
from jax.experimental import pallas as pl
from jax.experimental.pallas import tpu as pltpu
from jax.sharding import PartitionSpec as P

MESH = pl.DeviceIdType.MESH
BF = jnp.bfloat16
F32 = jnp.float32
BESIDE = ((-1, 0), (1, 0))
PIECES = ((1, -1, None), (1, 1, None), (0, -1, (0, 5)), (0, 1, (0, 5)), (-1, -1, None), (-1, 1, None),
          (0, -1, (5, 8)), (0, 1, (5, 8)), (-1, 0, None), (1, 0, None))
AROUND = ((-1, -1), (-1, 1), (1, -1), (1, 1), (0, -1), (0, 1)) + BESIDE


def iota(shape, axis):
    return lax.broadcasted_iota(jnp.int32, shape, axis)


def start(copy):
    copy.start()


def receive(copy):
    copy.wait_recv()


def sent(copy):
    copy.wait_send()


def choose(rows, target):
    return jnp.where(iota((rows, target.shape[1]), 0) == target, 1.0, 0.0).astype(BF)


def dot(a, b):
    return jnp.dot(a, b, preferred_element_type=F32)


def shifted(block, lane, low, high):
    zero = jnp.zeros_like(block)
    up = jnp.where(lane == low, zero, pltpu.roll(block, 1, 1))
    down = jnp.where(lane == high, zero, pltpu.roll(block, 127, 1))
    return up, down


def spread_one(w1, w1t):
    column = iota((1, 480), 1)
    own = column < 384
    edge = column & 31
    c = jnp.where(own, column >> 7, (column - 384) >> 5)
    y = jnp.where(own, column & 7, jnp.where(edge < 16, -1, 8))
    i = jnp.where(own, (column & 127) >> 3, column & 15)
    for out in range(8):
        b = y - out + 1
        target = jnp.where((b >= 0) & (b <= 2), 32 + b * 48 + c * 16 + i, -1)
        chosen = choose(176, target)
        row = (out % 2) * 128 + (out // 2) * 32
        for a, (start, skip) in enumerate(((0, 32), (128, 16), (256, 0))):
            part = dot(w1[:, start:144 * a + 144], chosen[skip:, :])
            w1t[a, row:row + 32, :] = part.astype(BF)


def spread_two(w2, w2t):
    column = iota((1, 576), 1)
    own = column < 384
    edge = column & 63
    c = jnp.where(own, column >> 7, (column - 384) >> 6)
    y = jnp.where(own, (column & 127) >> 5, jnp.where(edge < 32, -1, 4))
    i = column & 31
    for out in range(4):
        b = y - out + 1
        target = jnp.where((b >= 0) & (b <= 2), 64 + b * 96 + c * 32 + i, -1)
        chosen = choose(352, target)
        row = (out % 2) * 128 + (out // 2) * 64
        for a, (start, skip) in enumerate(((0, 64), (256, 32), (512, 0))):
            part = dot(w2[:, start:288 * a + 288], chosen[skip:, :])
            w2t[a, row:row + 64, :] = part.astype(BF)


def spread_three(shards, w3, w3t):
    column = iota((1, 384), 1)
    c = (column >= 128).astype(jnp.int32) + (column >= 256).astype(jnp.int32)
    pos = column - 128 * c
    y = pos >> 6
    i = pos & 63
    size = 128 // shards
    for t, outs in enumerate(((0, 2), (1, -1))):
        parts = [[], [], []]
        for out in outs:
            b = y - out + 1
            target = jnp.where((b >= 0) & (b <= 2), b * 192 + c * 64 + i, -1)
            chosen = choose(576, target)
            for a in range(3):
                parts[a].append(lax.dot_general(
                    w3[a * 576:(a + 1) * 576, :], chosen, (((0,), (0,)), ((), ())),
                    preferred_element_type=F32))
        for a in range(3):
            both = jnp.stack([p.reshape(shards, size, 384) for p in parts[a]], axis=1)
            w3t[t, :, a * 384:(a + 1) * 384] = both.reshape(256, 384).astype(BF)


def kernel(groups, shards, v_hbm, w1_hbm, w2_hbm, w3_hbm, o_ref,
           p, w1, w2, w3, face, b1, h1, a1, w1t, q, b2e, b2o, h2e, h2o, a2, w2t, w3t, out_s, in_s,
           load_sem, s1, r1, s2, r2, s3, r3, known):
    g = lax.axis_index("gx")
    s = lax.axis_index("yz")
    size = 128 // shards

    def at(dx, dy):
        return {"gx": lax.rem(g + dx + groups, groups), "yz": lax.rem(s + dy + shards, shards)}

    def has(dx, dy):
        x = {-1: g > 0, 0: None, 1: g < groups - 1}[dx]
        y = {-1: s > 0, 0: None, 1: s < shards - 1}[dy]
        return y if x is None else (x if y is None else x & y)

    def each(copies, act, sign, among=AROUND):
        for (dx, dy), copy in zip(AROUND, copies):
            if (dx, dy) in among:
                pl.when(has(sign * dx, sign * dy))(functools.partial(act, copy))

    def pieces(copies, act, sign, low, high):
        for (dx, dy, _), copy in zip(PIECES[low:high], copies[low:high]):
            pl.when(has(sign * dx, sign * dy))(functools.partial(act, copy))

    barrier = pltpu.get_barrier_semaphore()
    count = 0
    for dx, dy in AROUND:
        there = has(dx, dy)
        count = count + there.astype(jnp.int32)
        pl.when(there)(functools.partial(
            pl.semaphore_signal, barrier, inc=1, device_id=at(dx, dy), device_id_type=MESH))

    rounds = []
    while 2 << len(rounds) < shards:
        rounds.append(2 << len(rounds))

    def tell(r):
        for side, d in enumerate((-rounds[r], rounds[r])):
            pl.when((s + d >= 0) & (s + d < shards))(functools.partial(
                pl.semaphore_signal, known.at[r, side], inc=1,
                device_id={"gx": g, "yz": lax.rem(s + d + shards, shards)}, device_id_type=MESH))

    def hear(r):
        for side, d in enumerate((rounds[r], -rounds[r])):
            pl.when((s + d >= 0) & (s + d < shards))(functools.partial(
                pl.semaphore_wait, known.at[r, side], 1))

    loads = [
        pltpu.make_async_copy(v_hbm, p.at[1:9, 0:128], load_sem.at[0]),
        pltpu.make_async_copy(w1_hbm, w1, load_sem.at[1]),
        pltpu.make_async_copy(w2_hbm, w2, load_sem.at[2]),
        pltpu.make_async_copy(w3_hbm, w3, load_sem.at[3]),
    ]
    for load in loads:
        load.start()

    loads[0].wait()
    which = iota((32, 128), 0)
    ends = jnp.where(iota((32, 128), 1) == (which & 15) * 8 + (which >> 4) * 7, 1.0, 0.0).astype(BF)
    for x in range(0, 8, 2):
        cells = dot(ends, jnp.concatenate([p[1 + x, 0:128, :], p[2 + x, 0:128, :]], axis=1)).astype(BF)
        for k in range(2):
            face[0, x + k] = cells[0:16, k * 128:(k + 1) * 128]
            face[1, x + k] = cells[16:32, k * 128:(k + 1) * 128]

    @pl.when(g == 0)
    def _():
        p[0] = jnp.zeros((160, 128), BF)
        q[0:2] = jnp.zeros((2, 192, 128), BF)

    @pl.when(g == groups - 1)
    def _():
        p[9] = jnp.zeros((160, 128), BF)
        q[4:6] = jnp.zeros((2, 192, 128), BF)

    @pl.when(s == 0)
    def _():
        p[:, 128:144, :] = jnp.zeros((10, 16, 128), BF)
        q[:, 128:160, :] = jnp.zeros((6, 32, 128), BF)

    @pl.when(s == shards - 1)
    def _():
        p[:, 144:160, :] = jnp.zeros((10, 16, 128), BF)
        q[:, 160:192, :] = jnp.zeros((6, 32, 128), BF)

    pl.semaphore_wait(barrier, count)

    first = []
    for k, (dx, dy, part) in enumerate(PIECES):
        plane = 7 if dx > 0 else 0
        to = 0 if dx > 0 else 9
        side = 1 if dy > 0 else 0
        rows = slice(128, 144) if dy > 0 else slice(144, 160)
        if dy == 0:
            src, dst = p.at[1 + plane, 0:128], p.at[to, 0:128]
        elif dx == 0:
            low, high = part
            src, dst = face.at[side, low:high], p.at[1 + low:1 + high, rows]
        else:
            src, dst = face.at[side, plane], p.at[to, rows]
        first.append(pltpu.make_async_remote_copy(
            src_ref=src, dst_ref=dst, send_sem=s1.at[k], recv_sem=r1.at[k],
            device_id=at(dx, dy), device_id_type=MESH))
    pieces(first, start, 1, 0, 10)

    loads[1].wait()
    spread_one(w1, w1t)
    loads[2].wait()
    spread_two(w2, w2t)

    lane = iota((128, 128), 1)
    narrow = iota((32, 128), 1)

    def lay_one(x):
        mid = p[x, 0:128, :]
        up, down = shifted(mid, lane, 0, 127)
        b1[x, 0:128] = up
        b1[x, 128:256] = mid
        b1[x, 256:384] = down

    def two(ref, x):
        return jnp.concatenate([ref[x], ref[x + 1]], axis=1)

    for x in range(1, 9):
        lay_one(x)
    for k, taps in enumerate(((1, 2), (0, 1, 2), (0, 1, 2), (0, 1))):
        total = None
        for a in taps:
            part = dot(w1t[a, :, 0:384], two(b1, 2 * k + a))
            total = part if total is None else total + part
        a1[k] = total
    a1[0, :, 128:256] += dot(w1t[0, :, 0:384], b1[1])
    a1[3, :, 0:128] += dot(w1t[2, :, 0:384], b1[8])

    lanes = iota((256, 128), 1)
    pick = jnp.where(iota((256, 128), 0) == (lanes >> 6) * 128 + (lanes & 63) * 2, 1.0, 0.0).astype(BF)

    pieces(first, receive, -1, 8, 10)
    lay_one(0)
    lay_one(9)
    a1[0, :, 0:128] += dot(w1t[0, :, 0:384], b1[0])
    a1[3, :, 128:256] += dot(w1t[2, :, 0:384], b1[9])
    second = []
    for j in range(2):
        pieces(first, receive, -1, 4 * j, 4 * j + 4)
        for x in range(6 * j, 6 + 4 * j):
            mid = p[x, 128:160, :]
            up, down = shifted(mid, narrow, 0, 127)
            h1[x, 0:32] = up
            h1[x, 32:64] = mid
            h1[x, 64:96] = down
        pooled = []
        for k in (2 * j, 2 * j + 1):
            total = a1[k]
            for a in range(3):
                total += dot(w1t[a, :, 384:480], two(h1, 2 * k + a))
            total = jnp.maximum(total, 0.0)
            total = total[0:128] + total[128:256]
            total = total[:, 0:128] + total[:, 128:256]
            total = (total + pltpu.roll(total, 127, 1)) * 0.125
            pooled.append(total.astype(BF))
        q[2 + j, 0:128, :] = dot(jnp.concatenate(pooled, axis=1), pick).astype(BF)
        half = []
        for k, (dx, dy) in enumerate(AROUND):
            to = 2 + j - 2 * dx
            if dy == 0:
                rows, into = slice(0, 128), slice(0, 128)
            elif dy > 0:
                rows, into = slice(96, 128), slice(128, 160)
            else:
                rows, into = slice(0, 32), slice(160, 192)
            half.append(pltpu.make_async_remote_copy(
                src_ref=q.at[2 + j, rows], dst_ref=q.at[to, into], send_sem=s2.at[8 * j + k],
                recv_sem=r2.at[8 * j + k], device_id=at(dx, dy), device_id_type=MESH))
        each(half, start, 1)
        second.append(half)

    tell(0)
    loads[3].wait()
    spread_three(shards, w3, w3t)

    for r in range(len(rounds) - 1):
        hear(r)
        tell(r + 1)
    lane = iota((128, 128), 1) & 63
    low = iota((128, 128), 1) < 64

    def lay_two(even, odd, rows, size, lane, low):
        for j in range(5):
            if j > 0:
                mid = q[j, rows, :]
                up, down = shifted(mid, lane, 0, 63)
                even[j - 1, 0:size] = up
                even[j - 1, size:2 * size] = mid
                even[j - 1, 2 * size:3 * size] = down
            mid = jnp.where(low, pltpu.roll(q[j, rows, :], 64, 1), pltpu.roll(q[j + 1, rows, :], 64, 1))
            up, down = shifted(mid, lane, 0, 63)
            odd[j, 0:size] = up
            odd[j, size:2 * size] = mid
            odd[j, 2 * size:3 * size] = down

    def terms_two(even, odd, j, columns):
        total = dot(w2t[0, :, columns], two(odd, j))
        total += dot(w2t[1, :, columns], two(even, j))
        return total + dot(w2t[2, :, columns], two(odd, j + 1))

    column = iota((1, 384), 1)
    c = column >> 7
    inside = column & 127
    z = (inside & 31) + c - 1
    target = jnp.where((z >= 0) & (z < 32), (inside >> 6) * 64 + 2 * z, -1)
    chosen = choose(128, target)

    for half in second:
        each(half, receive, -1, BESIDE)
    lay_two(b2e, b2o, slice(0, 128), 128, lane, low)
    for j in range(2):
        a2[j] = terms_two(b2e, b2o, 2 * j, slice(0, 384))
    for half in second:
        each(half, receive, -1, AROUND[:6])
    lay_two(h2e, h2o, slice(128, 192), 64, lane[0:64], low[0:64])
    pooled = []
    for j in range(0, 4, 2):
        total = a2[j // 2] + terms_two(h2e, h2o, j, slice(384, 576))
        total = jnp.maximum(total, 0.0)
        total = total[0:128] + total[128:256]
        for k in range(2):
            pair = total[:, k * 128:(k + 1) * 128]
            pair = pair + pltpu.roll(pair, 64, 1)
            pair = (pair + pltpu.roll(pair, 127, 1)) * 0.125
            if j + k == 0:
                pair = jnp.where(g == 0, 0.0, pair)
            if j + k == 3:
                pair = jnp.where(g == groups - 1, 0.0, pair)
            pooled.append(pair)

    stacked = jnp.concatenate(
        [jnp.where(low, pooled[a], pooled[a + 1]).astype(BF) for a in range(3)], axis=0)
    planes = dot(stacked, chosen).astype(BF)
    right = jnp.concatenate(
        [planes[a * 128:(a + 1) * 128, c * 128:(c + 1) * 128] for a in range(3) for c in range(3)], axis=0)
    even = dot(w3t[0], right)
    odd = dot(w3t[1], right)
    parity = (iota((256, 128), 1) & 32) == 0
    out_s[...] = jnp.where(parity, even, odd).astype(BF).reshape(shards, 2 * size, 128)

    third = []
    deep = shards // 2
    far = sorted(range(deep), key=lambda d: -min(d, deep - d))
    for flip in (1, 0):
        for d in far:
            if (flip, d) == (0, 0):
                continue
            z = lax.rem(lax.div(s, 2) + d, deep)
            there = 2 * z + (1 - lax.rem(s, 2) if flip else lax.rem(s, 2))
            third.append(pltpu.make_async_remote_copy(
                src_ref=out_s.at[there], dst_ref=in_s.at[s], send_sem=s3.at[len(third)], recv_sem=r3.at[s],
                device_id={"gx": g, "yz": there}, device_id_type=MESH))
    hear(len(rounds) - 1)
    for copy in third:
        copy.start()
    in_s[s] = out_s[s]
    pieces(first, sent, 1, 0, 10)
    for half in second:
        each(half, sent, 1)

    low = iota((size, 128), 1) < 64
    parity = (iota((size, 128), 1) & 32) == 0
    nothing = jnp.zeros((size, 128), F32)
    main, cross = [], [nothing]
    for n in range(shards + 1):
        if n < shards:
            @pl.when(n != s)
            def _():
                pltpu.make_async_remote_copy(
                    src_ref=out_s.at[0], dst_ref=in_s.at[n], send_sem=s3.at[0], recv_sem=r3.at[n],
                    device_id=at(0, 1), device_id_type=MESH).wait_recv()
            block = in_s[n].astype(F32)
            main.append(block[0:size])
            cross.append(block[size:])
        else:
            cross.append(nothing)
        if n >= 2 and n % 2 == 0:
            left, right = [
                jnp.maximum(main[m] + jnp.where(parity, cross[m], cross[m + 2]), 0.0) for m in (n - 2, n - 1)]
            lanes = slice(n * 64 - 128, n * 64)
            at0 = jnp.where(low, left, pltpu.roll(right, 64, 1))
            at1 = jnp.where(low, pltpu.roll(left, 64, 1), right)
            o_ref[:, :, lanes] = jnp.stack([at0, at1], axis=1).astype(BF)
    for copy in third:
        copy.wait_send()


def per_device(volume, weight_one, weight_two, weight_three):
    groups, shards = lax.axis_size("gx"), lax.axis_size("yz")
    size = 128 // shards
    anywhere = pl.BlockSpec(memory_space=pl.ANY)
    dma = pltpu.SemaphoreType.DMA
    out = pl.pallas_call(
        functools.partial(kernel, groups, shards),
        out_shape=jax.ShapeDtypeStruct((size, 2, shards * 64), BF),
        in_specs=[anywhere] * 4,
        out_specs=pl.BlockSpec(memory_space=pltpu.VMEM),
        scratch_shapes=[
            pltpu.VMEM((10, 160, 128), BF),
            pltpu.VMEM((32, 432), BF),
            pltpu.VMEM((64, 864), BF),
            pltpu.VMEM((1728, 128), BF),
            pltpu.VMEM((2, 8, 16, 128), BF),
            pltpu.VMEM((10, 384, 128), BF),
            pltpu.VMEM((10, 96, 128), BF),
            pltpu.VMEM((4, 256, 256), F32),
            pltpu.VMEM((3, 256, 480), BF),
            pltpu.VMEM((6, 192, 128), BF),
            pltpu.VMEM((4, 384, 128), BF),
            pltpu.VMEM((5, 384, 128), BF),
            pltpu.VMEM((4, 192, 128), BF),
            pltpu.VMEM((5, 192, 128), BF),
            pltpu.VMEM((2, 256, 256), F32),
            pltpu.VMEM((3, 256, 576), BF),
            pltpu.VMEM((2, 256, 1152), BF),
            pltpu.VMEM((shards, 2 * size, 128), BF),
            pltpu.VMEM((shards, 2 * size, 128), BF),
            dma((4,)),
            dma((10,)), dma((10,)), dma((16,)), dma((16,)),
            dma((shards,)), dma((shards,)),
            pltpu.SemaphoreType.REGULAR((8, 2)),
        ],
        compiler_params=pltpu.CompilerParams(
            collective_id=0, has_side_effects=True, vmem_limit_bytes=56510000),
    )(volume.reshape(8, 128, 128), weight_one, weight_two, weight_three.T)
    return out


def solution(mesh):
    placed = (P("gx", None, "yz", None), P(), P(), P())
    return jax.shard_map(
        per_device, mesh=mesh, in_specs=placed, out_specs=P("yz", "gx", None), check_vma=False
    )
```

```python
import functools

import jax
import jax.numpy as jnp
from jax import lax
from jax.experimental import pallas as pl
from jax.experimental.pallas import tpu as pltpu
from jax.sharding import PartitionSpec as P

MESH = pl.DeviceIdType.MESH
BF = jnp.bfloat16
F32 = jnp.float32
BESIDE = ((-1, 0), (1, 0))
PIECES = ((1, -1, None), (1, 1, None), (0, -1, (0, 5)), (0, 1, (0, 5)), (-1, -1, None), (-1, 1, None),
          (0, -1, (5, 8)), (0, 1, (5, 8)), (-1, 0, None), (1, 0, None))
AROUND = ((-1, -1), (-1, 1), (1, -1), (1, 1), (0, -1), (0, 1)) + BESIDE


def iota(shape, axis):
    return lax.broadcasted_iota(jnp.int32, shape, axis)


def start(copy):
    copy.start()


def receive(copy):
    copy.wait_recv()


def sent(copy):
    copy.wait_send()


def choose(rows, target):
    return jnp.where(iota((rows, target.shape[1]), 0) == target, 1.0, 0.0).astype(BF)


def dot(a, b):
    return jnp.dot(a, b, preferred_element_type=F32)


def shifted(block, lane, low, high):
    zero = jnp.zeros_like(block)
    up = jnp.where(lane == low, zero, pltpu.roll(block, 1, 1))
    down = jnp.where(lane == high, zero, pltpu.roll(block, 127, 1))
    return up, down


def spread_one(w1, w1t):
    column = iota((1, 480), 1)
    own = column < 384
    edge = column & 31
    c = jnp.where(own, column >> 7, (column - 384) >> 5)
    y = jnp.where(own, column & 7, jnp.where(edge < 16, -1, 8))
    i = jnp.where(own, (column & 127) >> 3, column & 15)
    for out in range(8):
        b = y - out + 1
        target = jnp.where((b >= 0) & (b <= 2), 32 + b * 48 + c * 16 + i, -1)
        chosen = choose(176, target)
        row = (out % 2) * 128 + (out // 2) * 32
        for a, (start, skip) in enumerate(((0, 32), (128, 16), (256, 0))):
            part = dot(w1[:, start:144 * a + 144], chosen[skip:, :])
            w1t[a, row:row + 32, :] = part.astype(BF)


def spread_two(w2, w2t):
    column = iota((1, 576), 1)
    own = column < 384
    edge = column & 63
    c = jnp.where(own, column >> 7, (column - 384) >> 6)
    y = jnp.where(own, (column & 127) >> 5, jnp.where(edge < 32, -1, 4))
    i = column & 31
    for out in range(4):
        b = y - out + 1
        target = jnp.where((b >= 0) & (b <= 2), 64 + b * 96 + c * 32 + i, -1)
        chosen = choose(352, target)
        row = (out % 2) * 128 + (out // 2) * 64
        for a, (start, skip) in enumerate(((0, 64), (256, 32), (512, 0))):
            part = dot(w2[:, start:288 * a + 288], chosen[skip:, :])
            w2t[a, row:row + 64, :] = part.astype(BF)


def spread_three(shards, w3, w3t):
    column = iota((1, 384), 1)
    c = (column >= 128).astype(jnp.int32) + (column >= 256).astype(jnp.int32)
    pos = column - 128 * c
    y = pos >> 6
    i = pos & 63
    size = 128 // shards
    for t, outs in enumerate(((0, 2), (1, -1))):
        parts = [[], [], []]
        for out in outs:
            b = y - out + 1
            target = jnp.where((b >= 0) & (b <= 2), b * 192 + c * 64 + i, -1)
            chosen = choose(576, target)
            for a in range(3):
                parts[a].append(lax.dot_general(
                    w3[a * 576:(a + 1) * 576, :], chosen, (((0,), (0,)), ((), ())),
                    preferred_element_type=F32))
        for a in range(3):
            both = jnp.stack([p.reshape(shards, size, 384) for p in parts[a]], axis=1)
            w3t[t, :, a * 384:(a + 1) * 384] = both.reshape(256, 384).astype(BF)


def kernel(groups, shards, v_hbm, w1_hbm, w2_hbm, w3_hbm, o_ref,
           p, w1, w2, w3, face, b1, h1, a1, w1t, q, b2e, b2o, h2e, h2o, a2, w2t, w3t, out_s, in_s,
           load_sem, s1, r1, s2, r2, s3, r3, known):
    g = lax.axis_index("gx")
    s = lax.axis_index("yz")
    size = 128 // shards

    def at(dx, dy):
        return {"gx": lax.rem(g + dx + groups, groups), "yz": lax.rem(s + dy + shards, shards)}

    def has(dx, dy):
        x = {-1: g > 0, 0: None, 1: g < groups - 1}[dx]
        y = {-1: s > 0, 0: None, 1: s < shards - 1}[dy]
        return y if x is None else (x if y is None else x & y)

    def each(copies, act, sign, among=AROUND):
        for (dx, dy), copy in zip(AROUND, copies):
            if (dx, dy) in among:
                pl.when(has(sign * dx, sign * dy))(functools.partial(act, copy))

    def pieces(copies, act, sign, low, high):
        for (dx, dy, _), copy in zip(PIECES[low:high], copies[low:high]):
            pl.when(has(sign * dx, sign * dy))(functools.partial(act, copy))

    barrier = pltpu.get_barrier_semaphore()
    count = 0
    for dx, dy in AROUND:
        there = has(dx, dy)
        count = count + there.astype(jnp.int32)
        pl.when(there)(functools.partial(
            pl.semaphore_signal, barrier, inc=1, device_id=at(dx, dy), device_id_type=MESH))

    rounds = []
    while 2 << len(rounds) < shards:
        rounds.append(2 << len(rounds))

    def tell(r):
        for side, d in enumerate((-rounds[r], rounds[r])):
            pl.when((s + d >= 0) & (s + d < shards))(functools.partial(
                pl.semaphore_signal, known.at[r, side], inc=1,
                device_id={"gx": g, "yz": lax.rem(s + d + shards, shards)}, device_id_type=MESH))

    def hear(r):
        for side, d in enumerate((rounds[r], -rounds[r])):
            pl.when((s + d >= 0) & (s + d < shards))(functools.partial(
                pl.semaphore_wait, known.at[r, side], 1))

    loads = [
        pltpu.make_async_copy(v_hbm, p.at[1:9, 0:128], load_sem.at[0]),
        pltpu.make_async_copy(w1_hbm, w1, load_sem.at[1]),
        pltpu.make_async_copy(w2_hbm, w2, load_sem.at[2]),
        pltpu.make_async_copy(w3_hbm, w3, load_sem.at[3]),
    ]
    loads[0].start()

    loads[0].wait()
    for load in loads[1:]:
        load.start()
    which = iota((32, 128), 0)
    ends = jnp.where(iota((32, 128), 1) == (which & 15) * 8 + (which >> 4) * 7, 1.0, 0.0).astype(BF)
    for x in range(0, 8, 2):
        cells = dot(ends, jnp.concatenate([p[1 + x, 0:128, :], p[2 + x, 0:128, :]], axis=1)).astype(BF)
        for k in range(2):
            face[0, x + k] = cells[0:16, k * 128:(k + 1) * 128]
            face[1, x + k] = cells[16:32, k * 128:(k + 1) * 128]

    @pl.when(g == 0)
    def _():
        p[0] = jnp.zeros((160, 128), BF)
        q[0:2] = jnp.zeros((2, 192, 128), BF)

    @pl.when(g == groups - 1)
    def _():
        p[9] = jnp.zeros((160, 128), BF)
        q[4:6] = jnp.zeros((2, 192, 128), BF)

    @pl.when(s == 0)
    def _():
        p[:, 128:144, :] = jnp.zeros((10, 16, 128), BF)
        q[:, 128:160, :] = jnp.zeros((6, 32, 128), BF)

    @pl.when(s == shards - 1)
    def _():
        p[:, 144:160, :] = jnp.zeros((10, 16, 128), BF)
        q[:, 160:192, :] = jnp.zeros((6, 32, 128), BF)

    pl.semaphore_wait(barrier, count)

    first = []
    for k, (dx, dy, part) in enumerate(PIECES):
        plane = 7 if dx > 0 else 0
        to = 0 if dx > 0 else 9
        side = 1 if dy > 0 else 0
        rows = slice(128, 144) if dy > 0 else slice(144, 160)
        if dy == 0:
            src, dst = p.at[1 + plane, 0:128], p.at[to, 0:128]
        elif dx == 0:
            low, high = part
            src, dst = face.at[side, low:high], p.at[1 + low:1 + high, rows]
        else:
            src, dst = face.at[side, plane], p.at[to, rows]
        first.append(pltpu.make_async_remote_copy(
            src_ref=src, dst_ref=dst, send_sem=s1.at[k], recv_sem=r1.at[k],
            device_id=at(dx, dy), device_id_type=MESH))
    pieces(first, start, 1, 0, 10)

    loads[1].wait()
    spread_one(w1, w1t)
    loads[2].wait()
    spread_two(w2, w2t)

    lane = iota((128, 128), 1)
    narrow = iota((32, 128), 1)

    def lay_one(x):
        mid = p[x, 0:128, :]
        up, down = shifted(mid, lane, 0, 127)
        b1[x, 0:128] = up
        b1[x, 128:256] = mid
        b1[x, 256:384] = down

    def two(ref, x):
        return jnp.concatenate([ref[x], ref[x + 1]], axis=1)

    for x in range(1, 9):
        lay_one(x)
    for k, taps in enumerate(((1, 2), (0, 1, 2), (0, 1, 2), (0, 1))):
        total = None
        for a in taps:
            part = dot(w1t[a, :, 0:384], two(b1, 2 * k + a))
            total = part if total is None else total + part
        a1[k] = total
    a1[0, :, 128:256] += dot(w1t[0, :, 0:384], b1[1])
    a1[3, :, 0:128] += dot(w1t[2, :, 0:384], b1[8])

    lanes = iota((256, 128), 1)
    pick = jnp.where(iota((256, 128), 0) == (lanes >> 6) * 128 + (lanes & 63) * 2, 1.0, 0.0).astype(BF)

    pieces(first, receive, -1, 8, 10)
    lay_one(0)
    lay_one(9)
    a1[0, :, 0:128] += dot(w1t[0, :, 0:384], b1[0])
    a1[3, :, 128:256] += dot(w1t[2, :, 0:384], b1[9])
    second = []
    for j in range(2):
        pieces(first, receive, -1, 4 * j, 4 * j + 4)
        for x in range(6 * j, 6 + 4 * j):
            mid = p[x, 128:160, :]
            up, down = shifted(mid, narrow, 0, 127)
            h1[x, 0:32] = up
            h1[x, 32:64] = mid
            h1[x, 64:96] = down
        pooled = []
        for k in (2 * j, 2 * j + 1):
            total = a1[k]
            for a in range(3):
                total += dot(w1t[a, :, 384:480], two(h1, 2 * k + a))
            total = jnp.maximum(total, 0.0)
            total = total[0:128] + total[128:256]
            total = total[:, 0:128] + total[:, 128:256]
            total = (total + pltpu.roll(total, 127, 1)) * 0.125
            pooled.append(total.astype(BF))
        q[2 + j, 0:128, :] = dot(jnp.concatenate(pooled, axis=1), pick).astype(BF)
        half = []
        for k, (dx, dy) in enumerate(AROUND):
            to = 2 + j - 2 * dx
            if dy == 0:
                rows, into = slice(0, 128), slice(0, 128)
            elif dy > 0:
                rows, into = slice(96, 128), slice(128, 160)
            else:
                rows, into = slice(0, 32), slice(160, 192)
            half.append(pltpu.make_async_remote_copy(
                src_ref=q.at[2 + j, rows], dst_ref=q.at[to, into], send_sem=s2.at[8 * j + k],
                recv_sem=r2.at[8 * j + k], device_id=at(dx, dy), device_id_type=MESH))
        each(half, start, 1)
        second.append(half)

    tell(0)
    loads[3].wait()
    spread_three(shards, w3, w3t)

    for r in range(len(rounds) - 1):
        hear(r)
        tell(r + 1)
    lane = iota((128, 128), 1) & 63
    low = iota((128, 128), 1) < 64

    def lay_two(even, odd, rows, size, lane, low):
        for j in range(5):
            if j > 0:
                mid = q[j, rows, :]
                up, down = shifted(mid, lane, 0, 63)
                even[j - 1, 0:size] = up
                even[j - 1, size:2 * size] = mid
                even[j - 1, 2 * size:3 * size] = down
            mid = jnp.where(low, pltpu.roll(q[j, rows, :], 64, 1), pltpu.roll(q[j + 1, rows, :], 64, 1))
            up, down = shifted(mid, lane, 0, 63)
            odd[j, 0:size] = up
            odd[j, size:2 * size] = mid
            odd[j, 2 * size:3 * size] = down

    def terms_two(even, odd, j, columns):
        total = dot(w2t[0, :, columns], two(odd, j))
        total += dot(w2t[1, :, columns], two(even, j))
        return total + dot(w2t[2, :, columns], two(odd, j + 1))

    column = iota((1, 384), 1)
    c = column >> 7
    inside = column & 127
    z = (inside & 31) + c - 1
    target = jnp.where((z >= 0) & (z < 32), (inside >> 6) * 64 + 2 * z, -1)
    chosen = choose(128, target)

    for half in second:
        each(half, receive, -1, BESIDE)
    lay_two(b2e, b2o, slice(0, 128), 128, lane, low)
    for j in range(2):
        a2[j] = terms_two(b2e, b2o, 2 * j, slice(0, 384))
    for half in second:
        each(half, receive, -1, AROUND[:6])
    lay_two(h2e, h2o, slice(128, 192), 64, lane[0:64], low[0:64])
    pooled = []
    for j in range(0, 4, 2):
        total = a2[j // 2] + terms_two(h2e, h2o, j, slice(384, 576))
        total = jnp.maximum(total, 0.0)
        total = total[0:128] + total[128:256]
        for k in range(2):
            pair = total[:, k * 128:(k + 1) * 128]
            pair = pair + pltpu.roll(pair, 64, 1)
            pair = (pair + pltpu.roll(pair, 127, 1)) * 0.125
            if j + k == 0:
                pair = jnp.where(g == 0, 0.0, pair)
            if j + k == 3:
                pair = jnp.where(g == groups - 1, 0.0, pair)
            pooled.append(pair)

    stacked = jnp.concatenate(
        [jnp.where(low, pooled[a], pooled[a + 1]).astype(BF) for a in range(3)], axis=0)
    planes = dot(stacked, chosen).astype(BF)
    right = jnp.concatenate(
        [planes[a * 128:(a + 1) * 128, c * 128:(c + 1) * 128] for a in range(3) for c in range(3)], axis=0)
    even = dot(w3t[0], right)
    odd = dot(w3t[1], right)
    parity = (iota((256, 128), 1) & 32) == 0
    out_s[...] = jnp.where(parity, even, odd).astype(BF).reshape(shards, 2 * size, 128)

    third = []
    deep = shards // 2
    far = sorted(range(deep), key=lambda d: -min(d, deep - d))
    for flip in (1, 0):
        for d in far:
            if (flip, d) == (0, 0):
                continue
            z = lax.rem(lax.div(s, 2) + d, deep)
            there = 2 * z + (1 - lax.rem(s, 2) if flip else lax.rem(s, 2))
            third.append(pltpu.make_async_remote_copy(
                src_ref=out_s.at[there], dst_ref=in_s.at[s], send_sem=s3.at[len(third)], recv_sem=r3.at[s],
                device_id={"gx": g, "yz": there}, device_id_type=MESH))
    hear(len(rounds) - 1)
    for copy in third:
        copy.start()
    in_s[s] = out_s[s]
    pieces(first, sent, 1, 0, 10)
    for half in second:
        each(half, sent, 1)

    low = iota((size, 128), 1) < 64
    parity = (iota((size, 128), 1) & 32) == 0
    nothing = jnp.zeros((size, 128), F32)
    main, cross = [], [nothing]
    for n in range(shards + 1):
        if n < shards:
            @pl.when(n != s)
            def _():
                pltpu.make_async_remote_copy(
                    src_ref=out_s.at[0], dst_ref=in_s.at[n], send_sem=s3.at[0], recv_sem=r3.at[n],
                    device_id=at(0, 1), device_id_type=MESH).wait_recv()
            block = in_s[n].astype(F32)
            main.append(block[0:size])
            cross.append(block[size:])
        else:
            cross.append(nothing)
        if n >= 2 and n % 2 == 0:
            left, right = [
                jnp.maximum(main[m] + jnp.where(parity, cross[m], cross[m + 2]), 0.0) for m in (n - 2, n - 1)]
            lanes = slice(n * 64 - 128, n * 64)
            o_ref[0, :, lanes] = jnp.where(low, left, pltpu.roll(right, 64, 1)).astype(BF)
            o_ref[1, :, lanes] = jnp.where(low, pltpu.roll(left, 64, 1), right).astype(BF)
    for copy in third:
        copy.wait_send()


def per_device(volume, weight_one, weight_two, weight_three):
    groups, shards = lax.axis_size("gx"), lax.axis_size("yz")
    size = 128 // shards
    anywhere = pl.BlockSpec(memory_space=pl.ANY)
    dma = pltpu.SemaphoreType.DMA
    out = pl.pallas_call(
        functools.partial(kernel, groups, shards),
        out_shape=jax.ShapeDtypeStruct((2, size, shards * 64), BF),
        in_specs=[anywhere] * 4,
        out_specs=pl.BlockSpec(memory_space=pltpu.VMEM),
        scratch_shapes=[
            pltpu.VMEM((10, 160, 128), BF),
            pltpu.VMEM((32, 432), BF),
            pltpu.VMEM((64, 864), BF),
            pltpu.VMEM((1728, 128), BF),
            pltpu.VMEM((2, 8, 16, 128), BF),
            pltpu.VMEM((10, 384, 128), BF),
            pltpu.VMEM((10, 96, 128), BF),
            pltpu.VMEM((4, 256, 256), F32),
            pltpu.VMEM((3, 256, 480), BF),
            pltpu.VMEM((6, 192, 128), BF),
            pltpu.VMEM((4, 384, 128), BF),
            pltpu.VMEM((5, 384, 128), BF),
            pltpu.VMEM((4, 192, 128), BF),
            pltpu.VMEM((5, 192, 128), BF),
            pltpu.VMEM((2, 256, 256), F32),
            pltpu.VMEM((3, 256, 576), BF),
            pltpu.VMEM((2, 256, 1152), BF),
            pltpu.VMEM((shards, 2 * size, 128), BF),
            pltpu.VMEM((shards, 2 * size, 128), BF),
            dma((4,)),
            dma((10,)), dma((10,)), dma((16,)), dma((16,)),
            dma((shards,)), dma((shards,)),
            pltpu.SemaphoreType.REGULAR((8, 2)),
        ],
        compiler_params=pltpu.CompilerParams(
            collective_id=0, has_side_effects=True, vmem_limit_bytes=56510000),
    )(volume.reshape(8, 128, 128), weight_one, weight_two, weight_three.T)
    return jnp.moveaxis(out, 0, 1)


def solution(mesh):
    placed = (P("gx", None, "yz", None), P(), P(), P())
    return jax.shard_map(
        per_device, mesh=mesh, in_specs=placed, out_specs=P("yz", "gx", None), check_vma=False
    )
```
